32 devices in a mesh: az: 8 (over y, x, core), rad: 4 (over z).
Axes of the slice: x: 2, y: 2, z: 4, core: 2. Of those that a mesh axis runs over, the one named last changes fastest.
Arguments:
- plasma: float32 [8, 2, 32, 496], P(None, None, 'az', 'rad'), may hold values from -1.2 to 2, as said below
- shift_cells: int32 [496], replicated, may hold values from 0 to 31
- shift_fraction: int32 [496], replicated, may hold values from 0 to 255
- box_cells: int32 [1], replicated, may hold values from 0 to 31
- box_fraction: int32 [1], replicated, may hold values from 0 to 255
Outputs:
- advanced: float32 [8, 2, 32, 496], P(None, None, 'az', 'rad')
The draws below stay inside these ranges and needn't reach their ends.
Inputs may be any that keep to these rules, and one draw needn't show every extreme that they name: `plasma`: fields 0 and 4 lie in [0.5, 2]; the other fields lie in [-1.2, 1.2].
All inputs are finite; a program needn't handle non-finite values.
Results may differ from the reference program's by a relative error of at most 0.0003.
Values sent between devices are 32-bit elements; how exact they have to be, the bound alone decides.
A program may use at most 64 MiB of HBM per device.

```python
import jax
import jax.numpy as jnp
from jax import lax

CY = 4
NZ = 2
NX = 496
NY = 32
N_AZ = 8


def draw_plasma(key, part):
    keys = jax.random.split(jax.random.fold_in(key, 17), 4)
    full_shape = (NZ, NY, NX)
    density = jnp.exp(jax.random.uniform(keys[0], full_shape, jnp.float32, -0.69, 0.69))
    velocity = jnp.clip(0.3 * jax.random.normal(keys[1], (3,) + full_shape, jnp.float32), -1.2, 1.2)
    pressure = jnp.exp(jax.random.uniform(keys[2], full_shape, jnp.float32, -0.69, 0.69))
    magnetic = jnp.clip(0.3 * jax.random.normal(keys[3], (3,) + full_shape, jnp.float32), -1.2, 1.2)
    return jnp.concatenate([density[None], velocity, pressure[None], magnetic], axis=0)


def shear_total(key):
    keys = jax.random.split(jax.random.fold_in(key, 29), 2)
    slope_low = CY * 1024 // NX
    slope_high = CY * 8192 // NX + 1
    slope = jax.random.randint(keys[0], (), slope_low, slope_high, dtype=jnp.int32)
    offset = jax.random.randint(keys[1], (), 0, NY * 256, dtype=jnp.int32)
    rows = jnp.arange(NX, dtype=jnp.int32) - NX // 2
    return jnp.mod(offset + slope * rows, NY * 256).astype(jnp.int32)


def draw_shift_cells(key, part):
    return (shear_total(key) // 256).astype(jnp.int32)


def draw_shift_fraction(key, part):
    return jnp.mod(shear_total(key), 256).astype(jnp.int32)


def setup_inputs(seed: int = 0) -> dict:
    seeds = jax.random.split(jax.random.key(seed), 6)
    plasma = draw_plasma(jax.random.fold_in(seeds[5], 71), 0)
    shift_cells = draw_shift_cells(jax.random.fold_in(seeds[5], 71), 0)
    shift_fraction = draw_shift_fraction(jax.random.fold_in(seeds[5], 71), 0)
    box_cells = jax.random.randint(seeds[3], (1,), 0, NY).astype(jnp.int32)
    box_fraction = jax.random.randint(seeds[4], (1,), 0, 256).astype(jnp.int32)
    return dict(plasma=plasma, shift_cells=shift_cells, shift_fraction=shift_fraction, box_cells=box_cells, box_fraction=box_fraction)


gamma_ratio = 5.0 / 3.0
time_step = 0.05
spin_rate = 1.0
shear_rate = 1.5

def minmod(behind_diff, ahead_diff):
    return 0.5 * (jnp.sign(behind_diff) + jnp.sign(ahead_diff)) * jnp.minimum(jnp.abs(behind_diff), jnp.abs(ahead_diff))

def window(array, axis_pos, start_at, stop_at):
    return lax.slice_in_dim(array, start_at, stop_at, axis=axis_pos)

def limited_faces(quantity, axis_pos):
    extent = quantity.shape[axis_pos]
    differences = window(quantity, axis_pos, 1, extent) - window(quantity, axis_pos, 0, extent - 1)
    slopes = minmod(window(differences, axis_pos, 0, extent - 2), window(differences, axis_pos, 1, extent - 1))
    centre = window(quantity, axis_pos, 1, extent - 1)
    plus_side = centre + 0.5 * slopes
    minus_side = centre - 0.5 * slopes
    return (window(plus_side, axis_pos, 0, extent - 3), window(minus_side, axis_pos, 1, extent - 2))

def periodic_faces(quantity):
    ahead_diff = jnp.roll(quantity, -1, axis=0) - quantity
    behind_diff = quantity - jnp.roll(quantity, 1, axis=0)
    slopes = minmod(behind_diff, ahead_diff)
    return (jnp.roll(quantity + 0.5 * slopes, 1, axis=0), quantity - 0.5 * slopes)

def state_terms(primitive, normal_field):
    density, normal_vel, first_vel, second_vel, pressure, first_field, second_field = primitive
    field_sq = normal_field * normal_field + first_field * first_field + second_field * second_field
    total_press = pressure + 0.5 * field_sq
    energy = pressure / (gamma_ratio - 1.0) + 0.5 * density * (normal_vel * normal_vel + first_vel * first_vel + second_vel * second_vel) + 0.5 * field_sq
    vel_dot_field = normal_vel * normal_field + first_vel * first_field + second_vel * second_field
    normal_mom = density * normal_vel
    conserved = (density, normal_mom, density * first_vel, density * second_vel, energy, first_field, second_field)
    fluxes = (normal_mom, normal_mom * normal_vel + total_press - normal_field * normal_field, normal_mom * first_vel - normal_field * first_field, normal_mom * second_vel - normal_field * second_field, (energy + total_press) * normal_vel - normal_field * vel_dot_field, first_field * normal_vel - normal_field * first_vel, second_field * normal_vel - normal_field * second_vel)
    speed = jnp.abs(normal_vel) + jnp.sqrt((gamma_ratio * pressure + field_sq) / density)
    return (conserved, fluxes, speed)

def rusanov(left_state, right_state, normal_field):
    left_cons, left_flux, left_speed = state_terms(left_state, normal_field)
    right_cons, right_flux, right_speed = state_terms(right_state, normal_field)
    fastest = jnp.maximum(left_speed, right_speed)
    return tuple((0.5 * (left_flux[number] + right_flux[number]) - 0.5 * fastest * (right_cons[number] - left_cons[number]) for number in range(7)))

def advance(extended):
    density, radial_vel, azimuth_vel, vertical_vel, pressure, radial_face, azimuth_face, vertical_face = [extended[number] for number in range(8)]
    all_rows = extended.shape[2]
    all_cols = extended.shape[3]
    inner_rows = all_rows - 4
    inner_cols = all_cols - 4
    radial_centre = 0.5 * (radial_face[:, :, :-1] + radial_face[:, :, 1:])
    azimuth_centre = 0.5 * (azimuth_face[:, :-1, :] + azimuth_face[:, 1:, :])
    vertical_centre = 0.5 * (vertical_face + jnp.roll(vertical_face, -1, axis=0))
    mid_rows = slice(1, all_rows - 1)
    mid_cols = slice(1, all_cols - 1)
    radial_vars = (density[:, mid_rows], radial_vel[:, mid_rows], azimuth_vel[:, mid_rows], vertical_vel[:, mid_rows], pressure[:, mid_rows], azimuth_centre[:, mid_rows], vertical_centre[:, mid_rows])
    radial_pairs = [limited_faces(quantity, 2) for quantity in radial_vars]
    flux_radial = rusanov(tuple((pair[0] for pair in radial_pairs)), tuple((pair[1] for pair in radial_pairs)), radial_face[:, mid_rows, 2:all_cols - 1])
    azimuth_vars = (density[:, :, mid_cols], azimuth_vel[:, :, mid_cols], vertical_vel[:, :, mid_cols], radial_vel[:, :, mid_cols], pressure[:, :, mid_cols], vertical_centre[:, :, mid_cols], radial_centre[:, :, mid_cols])
    azimuth_pairs = [limited_faces(quantity, 1) for quantity in azimuth_vars]
    flux_azimuth = rusanov(tuple((pair[0] for pair in azimuth_pairs)), tuple((pair[1] for pair in azimuth_pairs)), azimuth_face[:, 2:all_rows - 1, mid_cols])
    vertical_vars = (density[:, mid_rows, mid_cols], vertical_vel[:, mid_rows, mid_cols], radial_vel[:, mid_rows, mid_cols], azimuth_vel[:, mid_rows, mid_cols], pressure[:, mid_rows, mid_cols], radial_centre[:, mid_rows, mid_cols], azimuth_centre[:, mid_rows, mid_cols])
    vertical_pairs = [periodic_faces(quantity) for quantity in vertical_vars]
    flux_vertical = rusanov(tuple((pair[0] for pair in vertical_pairs)), tuple((pair[1] for pair in vertical_pairs)), vertical_face[:, mid_rows, mid_cols])

    def radial_div(flux):
        return flux[:, 1:inner_rows + 1, 1:inner_cols + 1] - flux[:, 1:inner_rows + 1, 0:inner_cols]

    def azimuth_div(flux):
        return flux[:, 1:inner_rows + 1, 1:inner_cols + 1] - flux[:, 0:inner_rows, 1:inner_cols + 1]

    def vertical_div(flux):
        inside = flux[:, 1:inner_rows + 1, 1:inner_cols + 1]
        return jnp.roll(inside, -1, axis=0) - inside

    def total_div(radial_part, azimuth_part, vertical_part):
        return radial_div(flux_radial[radial_part]) + azimuth_div(flux_azimuth[azimuth_part]) + vertical_div(flux_vertical[vertical_part])
    cell_rows = slice(2, inner_rows + 2)
    cell_cols = slice(2, inner_cols + 2)
    cell_density = density[:, cell_rows, cell_cols]
    cell_radial = radial_vel[:, cell_rows, cell_cols]
    cell_azimuth = azimuth_vel[:, cell_rows, cell_cols]
    cell_vertical = vertical_vel[:, cell_rows, cell_cols]
    cell_pressure = pressure[:, cell_rows, cell_cols]
    centre_radial = radial_centre[:, cell_rows, cell_cols]
    centre_azimuth = azimuth_centre[:, cell_rows, cell_cols]
    centre_vertical = vertical_centre[:, cell_rows, cell_cols]
    cell_field_sq = centre_radial * centre_radial + centre_azimuth * centre_azimuth + centre_vertical * centre_vertical
    cell_energy = cell_pressure / (gamma_ratio - 1.0) + 0.5 * cell_density * (cell_radial * cell_radial + cell_azimuth * cell_azimuth + cell_vertical * cell_vertical) + 0.5 * cell_field_sq
    new_mass = cell_density - time_step * total_div(0, 0, 0)
    new_radial = cell_density * cell_radial - time_step * total_div(1, 3, 2) + time_step * 2.0 * spin_rate * cell_density * cell_azimuth
    new_azimuth = cell_density * cell_azimuth - time_step * total_div(2, 1, 3) - time_step * (2.0 - shear_rate) * spin_rate * cell_density * cell_radial
    new_vertical = cell_density * cell_vertical - time_step * total_div(3, 2, 1)
    new_energy = cell_energy - time_step * total_div(4, 4, 4)
    edge_vertical = 0.25 * (flux_azimuth[6][:, 0:inner_rows + 1, 1:inner_cols + 2] + flux_azimuth[6][:, 0:inner_rows + 1, 0:inner_cols + 1] - flux_radial[5][:, 1:inner_rows + 2, 0:inner_cols + 1] - flux_radial[5][:, 0:inner_rows + 1, 0:inner_cols + 1])
    radial_bz = flux_radial[6][:, 1:inner_rows + 1, 0:inner_cols + 1]
    edge_azimuth = 0.25 * (radial_bz + jnp.roll(radial_bz, 1, axis=0) - flux_vertical[5][:, 1:inner_rows + 1, 1:inner_cols + 2] - flux_vertical[5][:, 1:inner_rows + 1, 0:inner_cols + 1])
    azimuth_bz = flux_azimuth[5][:, 0:inner_rows + 1, 1:inner_cols + 1]
    edge_radial = 0.25 * (flux_vertical[6][:, 1:inner_rows + 2, 1:inner_cols + 1] + flux_vertical[6][:, 0:inner_rows + 1, 1:inner_cols + 1] - azimuth_bz - jnp.roll(azimuth_bz, 1, axis=0))
    new_radial_face = radial_face[:, cell_rows, cell_cols] - time_step * (edge_vertical[:, 1:inner_rows + 1, 0:inner_cols] - edge_vertical[:, 0:inner_rows, 0:inner_cols] - (jnp.roll(edge_azimuth, -1, axis=0)[:, :, 0:inner_cols] - edge_azimuth[:, :, 0:inner_cols]))
    new_azimuth_face = azimuth_face[:, cell_rows, cell_cols] - time_step * (jnp.roll(edge_radial, -1, axis=0)[:, 0:inner_rows] - edge_radial[:, 0:inner_rows] - (edge_vertical[:, 0:inner_rows, 1:inner_cols + 1] - edge_vertical[:, 0:inner_rows, 0:inner_cols]))
    new_vertical_face = vertical_face[:, cell_rows, cell_cols] - time_step * (edge_azimuth[:, :, 1:inner_cols + 1] - edge_azimuth[:, :, 0:inner_cols] - (edge_radial[:, 1:inner_rows + 1] - edge_radial[:, 0:inner_rows]))
    return jnp.stack([new_mass, new_radial, new_azimuth, new_vertical, new_energy, new_radial_face, new_azimuth_face, new_vertical_face], axis=0)

def extended_shifts(shift_cells, shift_fraction, box_cells, box_fraction, first_row, row_count, total_rows, total_cols):
    padded_cells = jnp.concatenate([shift_cells[total_rows - 2:], shift_cells, shift_cells[:2]])
    padded_fraction = jnp.concatenate([shift_fraction[total_rows - 2:], shift_fraction, shift_fraction[:2]])
    start_row = jnp.asarray(first_row).astype(jnp.int32)
    whole_cells = lax.dynamic_slice_in_dim(padded_cells, start_row, row_count + 4)
    whole_fraction = lax.dynamic_slice_in_dim(padded_fraction, start_row, row_count + 4)
    positions = start_row + jnp.arange(row_count + 4, dtype=jnp.int32) - 2
    below_box = (positions < 0).astype(jnp.int32)
    above_box = (positions >= total_rows).astype(jnp.int32)
    whole_cells = whole_cells + below_box * box_cells[0] + above_box * (total_cols - box_cells[0] - 1)
    whole_fraction = whole_fraction + below_box * box_fraction[0] + above_box * (256 - box_fraction[0])
    carry_over = whole_fraction // 256
    return (jnp.mod(whole_cells + carry_over, total_cols), whole_fraction - 256 * carry_over)

def reference(plasma, shift_cells, shift_fraction, box_cells, box_fraction):
    whole_cells, whole_fraction = extended_shifts(shift_cells, shift_fraction, box_cells, box_fraction, 0, NX, NX, NY)
    radial_ext = jnp.concatenate([plasma[:, :, :, NX - 2:], plasma, plasma[:, :, :, :2]], axis=3)
    weight_next = whole_fraction.astype(jnp.float32) * (1.0 / 256.0)
    weight_here = 1.0 - weight_next
    full_shape = (8, NZ, CY + 4, NX + 4)

    def one_block(block_index):
        targets = block_index * CY - 2 + jnp.arange(CY + 4, dtype=jnp.int32)
        sources = jnp.mod(targets[:, None] - whole_cells[None, :], NY).astype(jnp.int32)
        sources_next = jnp.mod(sources - 1, NY).astype(jnp.int32)
        here_val = jnp.take_along_axis(radial_ext, jnp.broadcast_to(sources, full_shape), axis=2)
        next_val = jnp.take_along_axis(radial_ext, jnp.broadcast_to(sources_next, full_shape), axis=2)
        return advance(weight_here * here_val + weight_next * next_val)
    blocks = lax.map(one_block, jnp.arange(N_AZ, dtype=jnp.int32))
    return jnp.transpose(blocks, (1, 2, 0, 3, 4)).reshape(8, NZ, NY, NX)
```

```python
import functools

import jax
import jax.numpy as jnp
from jax import lax
from jax.experimental import pallas as pl
from jax.experimental.pallas import tpu as pltpu
from jax.sharding import PartitionSpec as P

gamma_ratio = 5.0 / 3.0
time_step = 0.05
spin_rate = 1.0
shear_rate = 1.5
MESH = pl.DeviceIdType.MESH
LANES = 128
ROWS = 8


def minmod(a, b):
    return jnp.maximum(jnp.minimum(a, b), 0.0) + jnp.minimum(jnp.maximum(a, b), 0.0)


def before(x, axis):
    return pltpu.roll(x, 1, axis)


def after(x, axis):
    return pltpu.roll(x, x.shape[axis] - 1, axis)


def state_terms(primitive, normal_field):
    density, normal_vel, first_vel, second_vel, pressure, first_field, second_field = primitive
    field_sq = normal_field * normal_field + first_field * first_field + second_field * second_field
    total_press = pressure + 0.5 * field_sq
    normal_mom = density * normal_vel
    first_mom = density * first_vel
    second_mom = density * second_vel
    energy = (
        pressure * (1.0 / (gamma_ratio - 1.0))
        + 0.5 * (normal_mom * normal_vel + first_mom * first_vel + second_mom * second_vel)
        + 0.5 * field_sq
    )
    vel_dot_field = normal_vel * normal_field + first_vel * first_field + second_vel * second_field
    conserved = (density, normal_mom, first_mom, second_mom, energy, first_field, second_field)
    fluxes = (
        normal_mom,
        normal_mom * normal_vel + total_press - normal_field * normal_field,
        normal_mom * first_vel - normal_field * first_field,
        normal_mom * second_vel - normal_field * second_field,
        (energy + total_press) * normal_vel - normal_field * vel_dot_field,
        first_field * normal_vel - normal_field * first_vel,
        second_field * normal_vel - normal_field * second_vel,
    )
    speed = jnp.abs(normal_vel) + jnp.sqrt((gamma_ratio * pressure + field_sq) / density)
    return conserved, fluxes, speed


def rusanov(left_state, right_state, normal_field):
    left_cons, left_flux, left_speed = state_terms(left_state, normal_field)
    right_cons, right_flux, right_speed = state_terms(right_state, normal_field)
    half_fastest = 0.5 * jnp.maximum(left_speed, right_speed)
    return [
        0.5 * (lf + rf) - half_fastest * (rc - lc)
        for lf, rf, lc, rc in zip(left_flux, right_flux, left_cons, right_cons)
    ]


def limited(quantity, axis):
    diff = quantity - before(quantity, axis)
    half = 0.5 * minmod(diff, after(diff, axis))
    return before(quantity + half, axis), quantity - half


def advance(fields, planes):
    rho, vx, vy, vz, p, bx, by, bz = fields
    span = range(planes)
    up = [(z + 1) % planes for z in span]
    down = [(z - 1) % planes for z in span]
    cx = [0.5 * (bx[z] + after(bx[z], 1)) for z in span]
    cy = [0.5 * (by[z] + after(by[z], 0)) for z in span]
    cz = [0.5 * (bz[z] + bz[up[z]]) for z in span]

    def swept(group, axis, normal):
        out = []
        for z in span:
            pairs = [limited(quantity[z], axis) for quantity in group]
            out.append(rusanov([a for a, _ in pairs], [b for _, b in pairs], normal[z]))
        return out

    fx = swept((rho, vx, vy, vz, p, cy, cz), 1, bx)
    fy = swept((rho, vy, vz, vx, p, cz, cx), 0, by)
    group = (rho, vz, vx, vy, p, cx, cy)
    halves = [
        [0.5 * minmod(q[z] - q[down[z]], q[up[z]] - q[z]) for z in span] for q in group
    ]
    fz = [
        rusanov(
            [q[down[z]] + h[down[z]] for q, h in zip(group, halves)],
            [q[z] - h[z] for q, h in zip(group, halves)],
            bz[z],
        )
        for z in span
    ]

    ez = [
        0.25
        * (fy[z][6] + before(fy[z][6], 1) - fx[z][5] - before(fx[z][5], 0))
        for z in span
    ]
    ey = [
        0.25 * (fx[z][6] + fx[down[z]][6] - fz[z][5] - before(fz[z][5], 1)) for z in span
    ]
    ex = [
        0.25 * (fz[z][6] + before(fz[z][6], 0) - fy[z][5] - fy[down[z]][5]) for z in span
    ]
    result = []
    for z in span:
        def total_div(i, j, k):
            return (
                (after(fx[z][i], 1) - fx[z][i])
                + (after(fy[z][j], 0) - fy[z][j])
                + (fz[up[z]][k] - fz[z][k])
            )

        mx, my, mz = rho[z] * vx[z], rho[z] * vy[z], rho[z] * vz[z]
        energy = (
            p[z] * (1.0 / (gamma_ratio - 1.0))
            + 0.5 * (mx * vx[z] + my * vy[z] + mz * vz[z])
            + 0.5 * (cx[z] * cx[z] + cy[z] * cy[z] + cz[z] * cz[z])
        )
        result.append(
            (
                rho[z] - time_step * total_div(0, 0, 0),
                mx - time_step * total_div(1, 3, 2) + (time_step * 2.0 * spin_rate) * my,
                my
                - time_step * total_div(2, 1, 3)
                - (time_step * (2.0 - shear_rate) * spin_rate) * mx,
                mz - time_step * total_div(3, 2, 1),
                energy - time_step * total_div(4, 4, 4),
                bx[z] - time_step * (after(ez[z], 0) - ez[z] - (ey[up[z]] - ey[z])),
                by[z] - time_step * (ex[up[z]] - ex[z] - (after(ez[z], 1) - ez[z])),
                bz[z] - time_step * (after(ey[z], 1) - ey[z] - (after(ex[z], 0) - ex[z])),
            )
        )
    return result


def taken(x, index):
    return jnp.take_along_axis(x, index, axis=0, mode="promise_in_bounds")


def peer_order(n):
    if n & (n - 1):
        return None
    return sorted(range(1, n), key=lambda mask: (-(mask >> 1).bit_count(), mask))


def kernel(
    n, n_rad, planes, plasma_any, cells_any, fraction_any, box_cells_ref, box_fraction_ref, out_ref,
    block_ref, cells_ref, fraction_ref,
    gathered, from_low, from_high, packs, load_sem, send_sem, recv_sem, ready_sem,
):
    fields = block_ref.shape[0]
    strip = ROWS // planes
    row_count = plasma_any.shape[2]
    total_rows = cells_ref.shape[1]
    me, row = lax.axis_index("az"), lax.axis_index("rad")
    low, high = lax.rem(row + n_rad - 1, n_rad), lax.rem(row + 1, n_rad)
    order = peer_order(n) if n <= 16 else None

    def each(body):
        if order is not None:
            for mask in order:
                body(me ^ mask)
        else:
            lax.fori_loop(1, n, lambda step, _: (body(lax.rem(me + step, n)), 0)[1], 0)

    def every(body):
        each(body)
        body(me)

    loads = [
        pltpu.make_async_copy(source, target, load_sem.at[number])
        for number, (source, target) in enumerate(
            (
                (plasma_any, block_ref),
                (cells_any, cells_ref),
                (fraction_any, fraction_ref),
            )
        )
    ]
    for load in loads:
        load.start()

    barrier = pltpu.get_barrier_semaphore()

    def greet(device):
        pl.semaphore_signal(barrier, inc=1, device_id=device, device_id_type=MESH)

    each(lambda peer: greet((peer, row)))
    for beside in (low, high):

        @pl.when(beside > row)
        def _():
            every(lambda peer: greet((peer, beside)))

    lane = lax.broadcasted_iota(jnp.int32, (ROWS, LANES), 1)
    line = lax.broadcasted_iota(jnp.int32, (ROWS, LANES), 0)
    gathered[me] = jnp.zeros((fields, ROWS, LANES), jnp.float32)
    loads[0].wait()
    for f in range(fields):
        gathered[me, f, :, 0:row_count] = block_ref[f]
    block = [gathered[me, f] for f in range(fields)]
    to_low = jnp.zeros((ROWS, LANES), jnp.float32)
    to_high = jnp.zeros((ROWS, LANES), jnp.float32)
    for f in range(fields):
        at = (lane - 4 * f) & (LANES - 1)
        rolled = pltpu.roll(block[f], (LANES - 4 + 4 * f) % LANES, 1)
        to_low = jnp.where((at >= LANES - 4) & (at < LANES - 2), rolled, to_low)
        to_high = jnp.where(at >= LANES - 2, pltpu.roll(block[f], 4 + 4 * f, 1), to_high)
    packs[0] = to_low
    packs[1] = to_high

    earlier = (low < row).astype(jnp.int32) + (high < row).astype(jnp.int32)
    pl.semaphore_wait(barrier, n - 1 + n * earlier)

    def send(source, target, number, device):
        copy = pltpu.make_async_remote_copy(
            src_ref=source, dst_ref=target,
            send_sem=send_sem.at[number], recv_sem=recv_sem.at[number],
            device_id=device, device_id_type=MESH,
        )
        copy.start()
        return copy

    def send_low():
        every(lambda peer: send(packs.at[0], from_high.at[me], 0, (peer, low)))

    def send_high():
        every(lambda peer: send(packs.at[1], from_low.at[me], 1, (peer, high)))

    for number, beside in ((1, low), (0, high)):

        @pl.when(beside < row)
        def _():
            pl.semaphore_signal(
                ready_sem.at[number], inc=1, device_id=(me, beside), device_id_type=MESH
            )

    @pl.when(high < row)
    def _():
        send_high()

    @pl.when(low < row)
    def _():
        send_low()

    each(lambda peer: send(gathered.at[me], gathered.at[me], 2, (peer, row)))

    @pl.when(high > row)
    def _():
        pl.semaphore_wait(ready_sem.at[1], 1)
        send_high()

    @pl.when(low > row)
    def _():
        pl.semaphore_wait(ready_sem.at[0], 1)
        send_low()

    for load in loads[1:]:
        load.wait()
    cells_ref[...] = cells_ref[...] * 256 + fraction_ref[...]
    shifts = jnp.zeros((ROWS, LANES), jnp.int32)
    last = total_rows - LANES

    def loaded(start):
        return jnp.broadcast_to(cells_ref[:, start : start + LANES], (ROWS, LANES))

    for r in range(n_rad):
        start = r * row_count
        from_row = min(start, last)
        here = loaded(from_row)
        if start > from_row:
            here = pltpu.roll(here, LANES - (start - from_row), 1)
        ahead = (start + row_count) % total_rows
        behind = (start - 2) % total_rows
        for first_lane, first_row in ((row_count, ahead), (row_count + 2, behind)):
            begin = min(first_row, last)
            turn = (first_lane - (first_row - begin)) % LANES
            part = loaded(begin)
            part = pltpu.roll(part, turn, 1) if turn else part
            here = jnp.where(lane >= first_lane, part, here)
        shifts = jnp.where(row == r, here, shifts)
    box = box_cells_ref[0] * 256 + box_fraction_ref[0]
    circle = n * strip * 256
    below_box = (lane >= row_count + 2) & (row == 0)
    above_box = (lane >= row_count) & (lane < row_count + 2) & (row == n_rad - 1)
    shifts = shifts + jnp.where(below_box, box, 0) + jnp.where(above_box, circle - box, 0)
    shifts = jnp.where(shifts >= circle, shifts - circle, shifts)
    first = me * strip - 3 - (shifts >> 8)
    first = jnp.where(first < 0, first + n * strip, first)
    first = jnp.where(first < 0, first + n * strip, first)
    edge = lane >= row_count
    code = first * 256 + (shifts & 255)
    packed_code = jnp.where(edge, code, 0)
    for width in (4, 8, 16):
        packed_code = packed_code + pltpu.roll(packed_code, width, 1)
    mod_line = line & (strip - 1)
    early = line < strip

    def decoded(value):
        rows = value >> 8
        weight_next = (value & 255).astype(jnp.float32) * (1.0 / 256.0)
        return rows >> (strip.bit_length() - 1), rows & (strip - 1), weight_next

    device, inside, weight_next = decoded(code)
    packed_device, packed_inside, packed_weight = decoded(packed_code)
    in_low = (lane & 3) >= 2

    def arrived(ref, sem):
        pltpu.make_async_copy(ref, ref, sem).wait()

    others = pl.ds(0, n - 1)

    def chosen(count, where_from, load):
        def choose(e, state):
            values = load(e)
            out = []
            for d in range(3):
                hit = where_from == lax.rem(e + n - d, n)
                out.append([jnp.where(hit, v, h) for v, h in zip(values, state[d])])
            return out

        state = [[jnp.zeros((ROWS, LANES), jnp.float32)] * count for _ in range(3)]
        if n > 16:
            return lax.fori_loop(0, n, choose, state)
        for e in range(n):
            state = choose(e, state)
        return state

    def relocated(three, inside, weight_next):
        total = [None] * planes
        for weight, start in ((1.0 - weight_next, inside + 1), (weight_next, inside)):
            keep = mod_line >= start
            first = jnp.where(keep, three[0], three[1])
            second = jnp.where(keep, three[1], three[2])
            for z in range(planes):
                index = z * strip + ((line + start) & (strip - 1))
                part = weight * jnp.where(early, taken(first, index), taken(second, index))
                total[z] = part if total[z] is None else total[z] + part
        return total

    arrived(gathered.at[others], recv_sem.at[2])
    state = chosen(fields, device, lambda e: [gathered[e, f] for f in range(fields)])
    own = [relocated([s[f] for s in state], inside, weight_next) for f in range(fields)]

    arrived(from_low, recv_sem.at[1])
    arrived(from_high, recv_sem.at[0])
    state = chosen(1, packed_device, lambda e: [jnp.where(in_low, from_low[e], from_high[e])])
    halo = relocated([s[0] for s in state], packed_inside, packed_weight)
    shifted = [
        [
            jnp.where(edge, pltpu.roll(halo[z], (LANES - 4 * f) % LANES, 1), own[f][z])
            for z in range(planes)
        ]
        for f in range(fields)
    ]

    result = advance(shifted, planes)
    for f in range(fields):
        merged = pltpu.roll(result[0][f], ROWS - 2, 0)
        for z in range(1, planes):
            merged = jnp.where(
                line >= z * strip, pltpu.roll(result[z][f], (z * strip - 2) % ROWS, 0), merged
            )
        out_ref[f] = merged

    arrived(from_high, send_sem.at[0])
    arrived(from_low, send_sem.at[1])
    arrived(gathered.at[others], send_sem.at[2])


def body(plasma, shift_cells, shift_fraction, box_cells, box_fraction):
    fields, planes, strip, row_count = plasma.shape
    assert planes * strip == ROWS and strip + 4 == ROWS and row_count + 4 == LANES
    n, n_rad = lax.axis_size("az"), lax.axis_size("rad")
    total_rows = shift_cells.shape[0]
    block_shape = (fields, ROWS, row_count)
    out = pl.pallas_call(
        functools.partial(kernel, n, n_rad, planes),
        out_shape=pltpu.VMEM((fields, ROWS, LANES), jnp.float32),
        in_specs=[pl.BlockSpec(memory_space=pltpu.HBM)] * 3 + [pl.BlockSpec(memory_space=pltpu.SMEM)] * 2,
        out_specs=pl.BlockSpec(memory_space=pltpu.VMEM),
        scratch_shapes=[
            pltpu.VMEM(block_shape, jnp.float32),
            pltpu.VMEM((1, total_rows), jnp.int32),
            pltpu.VMEM((1, total_rows), jnp.int32),
            pltpu.VMEM((n, fields, ROWS, LANES), jnp.float32),
            pltpu.VMEM((n, ROWS, LANES), jnp.float32),
            pltpu.VMEM((n, ROWS, LANES), jnp.float32),
            pltpu.VMEM((2, ROWS, LANES), jnp.float32),
            pltpu.SemaphoreType.DMA((3,)),
            pltpu.SemaphoreType.DMA((3,)),
            pltpu.SemaphoreType.DMA((3,)),
            pltpu.SemaphoreType.REGULAR((2,)),
        ],
        compiler_params=pltpu.CompilerParams(collective_id=0, has_side_effects=True),
    )(
        plasma.reshape(block_shape),
        shift_cells.reshape(1, total_rows),
        shift_fraction.reshape(1, total_rows),
        box_cells,
        box_fraction,
    )
    return out[:, :, :row_count].reshape(plasma.shape)


def solution(mesh):
    placed = (P(None, None, "az", "rad"), P(), P(), P(), P())
    return jax.shard_map(
        body, mesh=mesh, in_specs=placed, out_specs=P(None, None, "az", "rad"), check_vma=False
    )
```

```python
import functools

import jax
import jax.numpy as jnp
from jax import lax
from jax.experimental import pallas as pl
from jax.experimental.pallas import tpu as pltpu
from jax.sharding import PartitionSpec as P

gamma_ratio = 5.0 / 3.0
time_step = 0.05
spin_rate = 1.0
shear_rate = 1.5
MESH = pl.DeviceIdType.MESH
LANES = 128
ROWS = 8


def minmod(a, b):
    return jnp.maximum(jnp.minimum(a, b), 0.0) + jnp.minimum(jnp.maximum(a, b), 0.0)


def before(x, axis):
    return pltpu.roll(x, 1, axis)


def after(x, axis):
    return pltpu.roll(x, x.shape[axis] - 1, axis)


def state_terms(primitive, normal_field):
    density, normal_vel, first_vel, second_vel, pressure, first_field, second_field = primitive
    field_sq = normal_field * normal_field + first_field * first_field + second_field * second_field
    total_press = pressure + 0.5 * field_sq
    normal_mom = density * normal_vel
    first_mom = density * first_vel
    second_mom = density * second_vel
    energy = (
        pressure * (1.0 / (gamma_ratio - 1.0))
        + 0.5 * (normal_mom * normal_vel + first_mom * first_vel + second_mom * second_vel)
        + 0.5 * field_sq
    )
    vel_dot_field = normal_vel * normal_field + first_vel * first_field + second_vel * second_field
    conserved = (density, normal_mom, first_mom, second_mom, energy, first_field, second_field)
    fluxes = (
        normal_mom,
        normal_mom * normal_vel + total_press - normal_field * normal_field,
        normal_mom * first_vel - normal_field * first_field,
        normal_mom * second_vel - normal_field * second_field,
        (energy + total_press) * normal_vel - normal_field * vel_dot_field,
        first_field * normal_vel - normal_field * first_vel,
        second_field * normal_vel - normal_field * second_vel,
    )
    speed = jnp.abs(normal_vel) + jnp.sqrt((gamma_ratio * pressure + field_sq) / density)
    return conserved, fluxes, speed


def rusanov(left_state, right_state, normal_field):
    left_cons, left_flux, left_speed = state_terms(left_state, normal_field)
    right_cons, right_flux, right_speed = state_terms(right_state, normal_field)
    half_fastest = 0.5 * jnp.maximum(left_speed, right_speed)
    return [
        0.5 * (lf + rf) - half_fastest * (rc - lc)
        for lf, rf, lc, rc in zip(left_flux, right_flux, left_cons, right_cons)
    ]


def limited(quantity, axis):
    diff = quantity - before(quantity, axis)
    half = 0.5 * minmod(diff, after(diff, axis))
    return before(quantity + half, axis), quantity - half


def advance(fields, planes):
    rho, vx, vy, vz, p, bx, by, bz = fields
    span = range(planes)
    up = [(z + 1) % planes for z in span]
    down = [(z - 1) % planes for z in span]
    cx = [0.5 * (bx[z] + after(bx[z], 1)) for z in span]
    cy = [0.5 * (by[z] + after(by[z], 0)) for z in span]
    cz = [0.5 * (bz[z] + bz[up[z]]) for z in span]

    def swept(group, axis, normal):
        out = []
        for z in span:
            pairs = [limited(quantity[z], axis) for quantity in group]
            out.append(rusanov([a for a, _ in pairs], [b for _, b in pairs], normal[z]))
        return out

    fx = swept((rho, vx, vy, vz, p, cy, cz), 1, bx)
    fy = swept((rho, vy, vz, vx, p, cz, cx), 0, by)
    group = (rho, vz, vx, vy, p, cx, cy)
    halves = [
        [0.5 * minmod(q[z] - q[down[z]], q[up[z]] - q[z]) for z in span] for q in group
    ]
    fz = [
        rusanov(
            [q[down[z]] + h[down[z]] for q, h in zip(group, halves)],
            [q[z] - h[z] for q, h in zip(group, halves)],
            bz[z],
        )
        for z in span
    ]

    ez = [
        0.25
        * (fy[z][6] + before(fy[z][6], 1) - fx[z][5] - before(fx[z][5], 0))
        for z in span
    ]
    ey = [
        0.25 * (fx[z][6] + fx[down[z]][6] - fz[z][5] - before(fz[z][5], 1)) for z in span
    ]
    ex = [
        0.25 * (fz[z][6] + before(fz[z][6], 0) - fy[z][5] - fy[down[z]][5]) for z in span
    ]
    result = []
    for z in span:
        def total_div(i, j, k):
            return (
                (after(fx[z][i], 1) - fx[z][i])
                + (after(fy[z][j], 0) - fy[z][j])
                + (fz[up[z]][k] - fz[z][k])
            )

        mx, my, mz = rho[z] * vx[z], rho[z] * vy[z], rho[z] * vz[z]
        energy = (
            p[z] * (1.0 / (gamma_ratio - 1.0))
            + 0.5 * (mx * vx[z] + my * vy[z] + mz * vz[z])
            + 0.5 * (cx[z] * cx[z] + cy[z] * cy[z] + cz[z] * cz[z])
        )
        result.append(
            (
                rho[z] - time_step * total_div(0, 0, 0),
                mx - time_step * total_div(1, 3, 2) + (time_step * 2.0 * spin_rate) * my,
                my
                - time_step * total_div(2, 1, 3)
                - (time_step * (2.0 - shear_rate) * spin_rate) * mx,
                mz - time_step * total_div(3, 2, 1),
                energy - time_step * total_div(4, 4, 4),
                bx[z] - time_step * (after(ez[z], 0) - ez[z] - (ey[up[z]] - ey[z])),
                by[z] - time_step * (ex[up[z]] - ex[z] - (after(ez[z], 1) - ez[z])),
                bz[z] - time_step * (after(ey[z], 1) - ey[z] - (after(ex[z], 0) - ex[z])),
            )
        )
    return result


def taken(x, index):
    return jnp.take_along_axis(x, index, axis=0, mode="promise_in_bounds")


def kernel(
    n, n_rad, planes, plasma_any, cells_any, fraction_any, box_ref, out_ref,
    block_ref, cells_ref, fraction_ref,
    gathered, from_low, from_high, packs, load_sem, send_sem, recv_sem,
    ready_sem, line_sem, edge_ref,
):
    fields = block_ref.shape[0]
    strip = ROWS // planes
    row_count = plasma_any.shape[2]
    total_rows = cells_ref.shape[1]
    me, row = lax.axis_index("az"), lax.axis_index("rad")
    low, high = lax.rem(row + n_rad - 1, n_rad), lax.rem(row + 1, n_rad)

    def over(first, last, body):
        lax.fori_loop(first, last, lambda peer, _: (body(peer), 0)[1], 0)

    def everywhere(body):
        if n <= 16:
            for peer in range(n):
                body(peer)
        else:
            over(0, n, body)

    loads = [
        pltpu.make_async_copy(source, target, load_sem.at[number])
        for number, (source, target) in enumerate(
            (
                (plasma_any, block_ref),
                (cells_any, cells_ref),
                (fraction_any, fraction_ref),
            )
        )
    ]
    for load in loads:
        load.start()

    barrier = pltpu.get_barrier_semaphore()

    def greet(device):
        pl.semaphore_signal(barrier, inc=1, device_id=device, device_id_type=MESH)

    for beside in (low, high):

        @pl.when(beside > row)
        def _():
            everywhere(lambda peer: greet((peer, beside)))

    over(me + 1, n, lambda peer: greet((peer, row)))

    lane = lax.broadcasted_iota(jnp.int32, (ROWS, LANES), 1)
    line = lax.broadcasted_iota(jnp.int32, (ROWS, LANES), 0)
    box = jnp.broadcast_to(box_ref[...], (ROWS, LANES))
    for f in range(fields):
        gathered[me, f] = box
    loads[0].wait()
    for f in range(fields):
        gathered[me, f, :, 0:row_count] = block_ref[f]
    block = [gathered[me, f] for f in range(fields)]
    to_low = box
    to_high = jnp.zeros((ROWS, LANES), jnp.float32)
    for f in range(fields):
        at = (lane - 4 * f) & (LANES - 1)
        rolled = pltpu.roll(block[f], (LANES - 4 + 4 * f) % LANES, 1)
        to_low = jnp.where((at >= LANES - 4) & (at < LANES - 2), rolled, to_low)
        to_high = jnp.where(at >= LANES - 2, pltpu.roll(block[f], 4 + 4 * f, 1), to_high)
    packs[0] = to_low
    packs[1] = to_high

    earlier = (low < row).astype(jnp.int32) + (high < row).astype(jnp.int32)
    greetings = me + n * earlier

    @pl.when(greetings > 0)
    def _():
        pl.semaphore_wait(barrier, greetings)

    def tell(semaphore, device):
        pl.semaphore_signal(semaphore, inc=1, device_id=device, device_id_type=MESH)

    def send(source, target, number, device):
        pltpu.make_async_remote_copy(
            src_ref=source, dst_ref=target,
            send_sem=send_sem.at[number], recv_sem=recv_sem.at[number],
            device_id=device, device_id_type=MESH,
        ).start()

    def send_low():
        everywhere(lambda peer: send(packs.at[0], from_high.at[me], 0, (peer, low)))

    def send_high():
        everywhere(lambda peer: send(packs.at[1], from_low.at[me], 1, (peer, high)))

    def send_block(peer):
        send(gathered.at[me], gathered.at[me], 2, (peer, row))

    def send_block_later(peer):
        pl.semaphore_wait(line_sem.at[peer], 1)
        send_block(peer)

    for number, beside in ((1, low), (0, high)):

        @pl.when((beside < row) & (me == n - 1))
        def _():
            everywhere(lambda peer: tell(ready_sem.at[number], (peer, beside)))

    @pl.when(high < row)
    def _():
        send_high()

    @pl.when(low < row)
    def _():
        send_low()

    over(0, me, lambda peer: tell(line_sem.at[me], (peer, row)))
    over(0, me, send_block)

    for load in loads[1:]:
        load.wait()
    cells_ref[...] = cells_ref[...] * 256 + fraction_ref[...]
    shifts = jnp.zeros((ROWS, LANES), jnp.int32)
    last = total_rows - LANES

    def loaded(start):
        return jnp.broadcast_to(cells_ref[:, start : start + LANES], (ROWS, LANES))

    for r in range(n_rad):
        start = r * row_count
        from_row = min(start, last)
        here = loaded(from_row)
        if start > from_row:
            here = pltpu.roll(here, LANES - (start - from_row), 1)
        ahead = (start + row_count) % total_rows
        behind = (start - 2) % total_rows
        for first_lane, first_row in ((row_count, ahead), (row_count + 2, behind)):
            begin = min(first_row, last)
            turn = (first_lane - (first_row - begin)) % LANES
            part = loaded(begin)
            part = pltpu.roll(part, turn, 1) if turn else part
            here = jnp.where(lane >= first_lane, part, here)
        shifts = jnp.where(row == r, here, shifts)
    circle = n * strip * 256
    below_box = (lane >= row_count + 2) & (row == 0)
    above_box = (lane >= row_count) & (lane < row_count + 2) & (row == n_rad - 1)
    edge = lane >= row_count

    def coded(total):
        total = jnp.where(total >= circle, total - circle, total)
        first = me * strip - 3 - (total >> 8)
        first = jnp.where(first < 0, first + n * strip, first)
        first = jnp.where(first < 0, first + n * strip, first)
        return first * 256 + (total & 255)

    def code_edges(offset):
        offset = offset.astype(jnp.int32)
        total = shifts + jnp.where(below_box, offset, 0) + jnp.where(above_box, circle - offset, 0)
        packed = jnp.where(edge, coded(total), 0)
        for width in (4, 8, 16):
            packed = packed + pltpu.roll(packed, width, 1)
        edge_ref[...] = packed

    mod_line = line & (strip - 1)
    early = line < strip

    def decoded(value):
        rows = value >> 8
        weight_next = (value & 255).astype(jnp.float32) * (1.0 / 256.0)
        return rows >> (strip.bit_length() - 1), rows & (strip - 1), weight_next

    device, inside, weight_next = decoded(coded(shifts))
    in_low = (lane & 3) >= 2

    def arrived(ref, sem):
        pltpu.make_async_copy(ref, ref, sem).wait()

    over(me + 1, n, send_block_later)

    @pl.when(high > row)
    def _():
        pl.semaphore_wait(ready_sem.at[1], 1)
        send_high()

    @pl.when(low > row)
    def _():
        pl.semaphore_wait(ready_sem.at[0], 1)
        send_low()

    others = pl.ds(0, n - 1)

    def chosen(count, where_from, load):
        def choose(e, state):
            values = load(e)
            out = []
            for d in range(3):
                hit = where_from == lax.rem(e + n - d, n)
                out.append([jnp.where(hit, v, h) for v, h in zip(values, state[d])])
            return out

        state = [[jnp.zeros((ROWS, LANES), jnp.float32)] * count for _ in range(3)]
        if n > 16:
            return lax.fori_loop(0, n, choose, state)
        for e in range(n):
            state = choose(e, state)
        return state

    def relocated(three, inside, weight_next):
        total = [None] * planes
        for weight, start in ((1.0 - weight_next, inside + 1), (weight_next, inside)):
            keep = mod_line >= start
            first = jnp.where(keep, three[0], three[1])
            second = jnp.where(keep, three[1], three[2])
            for z in range(planes):
                index = z * strip + ((line + start) & (strip - 1))
                part = weight * jnp.where(early, taken(first, index), taken(second, index))
                total[z] = part if total[z] is None else total[z] + part
        return total

    arrived(gathered.at[others], recv_sem.at[2])

    @pl.when(row != n_rad - 1)
    def _():
        code_edges(gathered[0, 0])

    state = chosen(fields, device, lambda e: [gathered[e, f] for f in range(fields)])
    own = [relocated([s[f] for s in state], inside, weight_next) for f in range(fields)]

    arrived(from_low, recv_sem.at[1])
    arrived(from_high, recv_sem.at[0])

    @pl.when(row == n_rad - 1)
    def _():
        code_edges(pltpu.roll(from_high[0], LANES // 2, 1))

    packed_device, packed_inside, packed_weight = decoded(edge_ref[...])
    state = chosen(1, packed_device, lambda e: [jnp.where(in_low, from_low[e], from_high[e])])
    halo = relocated([s[0] for s in state], packed_inside, packed_weight)
    shifted = [
        [
            jnp.where(edge, pltpu.roll(halo[z], (LANES - 4 * f) % LANES, 1), own[f][z])
            for z in range(planes)
        ]
        for f in range(fields)
    ]

    result = advance(shifted, planes)
    for f in range(fields):
        merged = pltpu.roll(result[0][f], ROWS - 2, 0)
        for z in range(1, planes):
            merged = jnp.where(
                line >= z * strip, pltpu.roll(result[z][f], (z * strip - 2) % ROWS, 0), merged
            )
        out_ref[f] = merged

    arrived(from_high, send_sem.at[0])
    arrived(from_low, send_sem.at[1])
    arrived(gathered.at[others], send_sem.at[2])


def body(plasma, shift_cells, shift_fraction, box_cells, box_fraction):
    fields, planes, strip, row_count = plasma.shape
    assert planes * strip == ROWS and strip + 4 == ROWS and row_count + 4 == LANES
    n, n_rad = lax.axis_size("az"), lax.axis_size("rad")
    total_rows = shift_cells.shape[0]
    block_shape = (fields, ROWS, row_count)
    box = lax.cond(
        (lax.axis_index("az") == 0) & (lax.axis_index("rad") == 0),
        lambda cells, fraction: jnp.broadcast_to(cells * 256 + fraction, (LANES,)).astype(jnp.float32),
        lambda cells, fraction: jnp.zeros((LANES,), jnp.float32),
        box_cells, box_fraction,
    )
    out = pl.pallas_call(
        functools.partial(kernel, n, n_rad, planes),
        out_shape=pltpu.VMEM((fields, ROWS, LANES), jnp.float32),
        in_specs=[pl.BlockSpec(memory_space=pltpu.HBM)] * 3 + [pl.BlockSpec(memory_space=pltpu.VMEM)],
        out_specs=pl.BlockSpec(memory_space=pltpu.VMEM),
        scratch_shapes=[
            pltpu.VMEM(block_shape, jnp.float32),
            pltpu.VMEM((1, total_rows), jnp.int32),
            pltpu.VMEM((1, total_rows), jnp.int32),
            pltpu.VMEM((n, fields, ROWS, LANES), jnp.float32),
            pltpu.VMEM((n, ROWS, LANES), jnp.float32),
            pltpu.VMEM((n, ROWS, LANES), jnp.float32),
            pltpu.VMEM((2, ROWS, LANES), jnp.float32),
            pltpu.SemaphoreType.DMA((3,)),
            pltpu.SemaphoreType.DMA((3,)),
            pltpu.SemaphoreType.DMA((3,)),
            pltpu.SemaphoreType.REGULAR((2,)),
            pltpu.SemaphoreType.REGULAR((n,)),
            pltpu.VMEM((ROWS, LANES), jnp.int32),
        ],
        compiler_params=pltpu.CompilerParams(collective_id=0, has_side_effects=True),
    )(
        plasma.reshape(block_shape),
        shift_cells.reshape(1, total_rows),
        shift_fraction.reshape(1, total_rows),
        box.reshape(1, LANES),
    )
    return out[:, :, :row_count].reshape(plasma.shape)


def solution(mesh):
    placed = (P(None, None, "az", "rad"), P(), P(), P(), P())
    return jax.shard_map(
        body, mesh=mesh, in_specs=placed, out_specs=P(None, None, "az", "rad"), check_vma=False
    )
```

```python
import functools

import jax
import jax.numpy as jnp
from jax import lax
from jax.experimental import pallas as pl
from jax.experimental.pallas import tpu as pltpu
from jax.sharding import PartitionSpec as P

gamma_ratio = 5.0 / 3.0
time_step = 0.05
spin_rate = 1.0
shear_rate = 1.5
MESH = pl.DeviceIdType.MESH
LANES = 128
ROWS = 8


def minmod(a, b):
    return jnp.maximum(jnp.minimum(a, b), 0.0) + jnp.minimum(jnp.maximum(a, b), 0.0)


def before(x, axis):
    return pltpu.roll(x, 1, axis)


def after(x, axis):
    return pltpu.roll(x, x.shape[axis] - 1, axis)


def state_terms(primitive, normal_field):
    density, normal_vel, first_vel, second_vel, pressure, first_field, second_field = primitive
    field_sq = normal_field * normal_field + first_field * first_field + second_field * second_field
    total_press = pressure + 0.5 * field_sq
    normal_mom = density * normal_vel
    first_mom = density * first_vel
    second_mom = density * second_vel
    energy = (
        pressure * (1.0 / (gamma_ratio - 1.0))
        + 0.5 * (normal_mom * normal_vel + first_mom * first_vel + second_mom * second_vel)
        + 0.5 * field_sq
    )
    vel_dot_field = normal_vel * normal_field + first_vel * first_field + second_vel * second_field
    conserved = (density, normal_mom, first_mom, second_mom, energy, first_field, second_field)
    fluxes = (
        normal_mom,
        normal_mom * normal_vel + total_press - normal_field * normal_field,
        normal_mom * first_vel - normal_field * first_field,
        normal_mom * second_vel - normal_field * second_field,
        (energy + total_press) * normal_vel - normal_field * vel_dot_field,
        first_field * normal_vel - normal_field * first_vel,
        second_field * normal_vel - normal_field * second_vel,
    )
    speed = jnp.abs(normal_vel) + jnp.sqrt((gamma_ratio * pressure + field_sq) / density)
    return conserved, fluxes, speed


def rusanov(left_state, right_state, normal_field):
    left_cons, left_flux, left_speed = state_terms(left_state, normal_field)
    right_cons, right_flux, right_speed = state_terms(right_state, normal_field)
    half_fastest = 0.5 * jnp.maximum(left_speed, right_speed)
    return [
        0.5 * (lf + rf) - half_fastest * (rc - lc)
        for lf, rf, lc, rc in zip(left_flux, right_flux, left_cons, right_cons)
    ]


def limited(quantity, axis):
    diff = quantity - before(quantity, axis)
    half = 0.5 * minmod(diff, after(diff, axis))
    return before(quantity + half, axis), quantity - half


def advance(fields, planes):
    rho, vx, vy, vz, p, bx, by, bz = fields
    span = range(planes)
    up = [(z + 1) % planes for z in span]
    down = [(z - 1) % planes for z in span]
    cx = [0.5 * (bx[z] + after(bx[z], 1)) for z in span]
    cy = [0.5 * (by[z] + after(by[z], 0)) for z in span]
    cz = [0.5 * (bz[z] + bz[up[z]]) for z in span]

    def swept(group, axis, normal):
        out = []
        for z in span:
            pairs = [limited(quantity[z], axis) for quantity in group]
            out.append(rusanov([a for a, _ in pairs], [b for _, b in pairs], normal[z]))
        return out

    fx = swept((rho, vx, vy, vz, p, cy, cz), 1, bx)
    fy = swept((rho, vy, vz, vx, p, cz, cx), 0, by)
    group = (rho, vz, vx, vy, p, cx, cy)
    halves = [
        [0.5 * minmod(q[z] - q[down[z]], q[up[z]] - q[z]) for z in span] for q in group
    ]
    fz = [
        rusanov(
            [q[down[z]] + h[down[z]] for q, h in zip(group, halves)],
            [q[z] - h[z] for q, h in zip(group, halves)],
            bz[z],
        )
        for z in span
    ]

    ez = [
        0.25
        * (fy[z][6] + before(fy[z][6], 1) - fx[z][5] - before(fx[z][5], 0))
        for z in span
    ]
    ey = [
        0.25 * (fx[z][6] + fx[down[z]][6] - fz[z][5] - before(fz[z][5], 1)) for z in span
    ]
    ex = [
        0.25 * (fz[z][6] + before(fz[z][6], 0) - fy[z][5] - fy[down[z]][5]) for z in span
    ]
    result = []
    for z in span:
        def total_div(i, j, k):
            return (
                (after(fx[z][i], 1) - fx[z][i])
                + (after(fy[z][j], 0) - fy[z][j])
                + (fz[up[z]][k] - fz[z][k])
            )

        mx, my, mz = rho[z] * vx[z], rho[z] * vy[z], rho[z] * vz[z]
        energy = (
            p[z] * (1.0 / (gamma_ratio - 1.0))
            + 0.5 * (mx * vx[z] + my * vy[z] + mz * vz[z])
            + 0.5 * (cx[z] * cx[z] + cy[z] * cy[z] + cz[z] * cz[z])
        )
        result.append(
            (
                rho[z] - time_step * total_div(0, 0, 0),
                mx - time_step * total_div(1, 3, 2) + (time_step * 2.0 * spin_rate) * my,
                my
                - time_step * total_div(2, 1, 3)
                - (time_step * (2.0 - shear_rate) * spin_rate) * mx,
                mz - time_step * total_div(3, 2, 1),
                energy - time_step * total_div(4, 4, 4),
                bx[z] - time_step * (after(ez[z], 0) - ez[z] - (ey[up[z]] - ey[z])),
                by[z] - time_step * (ex[up[z]] - ex[z] - (after(ez[z], 1) - ez[z])),
                bz[z] - time_step * (after(ey[z], 1) - ey[z] - (after(ex[z], 0) - ex[z])),
            )
        )
    return result


def taken(x, index):
    return jnp.take_along_axis(x, index, axis=0, mode="promise_in_bounds")


def kernel(
    n, n_rad, planes, plasma_any, cells_any, fraction_any, box_ref, out_ref,
    block_ref, cells_ref, fraction_ref,
    gathered, from_low, from_high, packs, load_sem, send_sem, recv_sem,
    ready_sem, line_sem, near_sem, edge_ref,
):
    fields = block_ref.shape[0]
    strip = ROWS // planes
    row_count = plasma_any.shape[2]
    total_rows = cells_ref.shape[1]
    me, row = lax.axis_index("az"), lax.axis_index("rad")
    low, high = lax.rem(row + n_rad - 1, n_rad), lax.rem(row + 1, n_rad)

    def over(first, last, body):
        lax.fori_loop(first, last, lambda peer, _: (body(peer), 0)[1], 0)

    def everywhere(body):
        if n <= 16:
            for peer in range(n):
                body(peer)
        else:
            over(0, n, body)

    loads = [
        pltpu.make_async_copy(source, target, load_sem.at[number])
        for number, (source, target) in enumerate(
            (
                (plasma_any, block_ref),
                (cells_any, cells_ref),
                (fraction_any, fraction_ref),
            )
        )
    ]
    for load in loads:
        load.start()

    barrier = pltpu.get_barrier_semaphore()

    def greet(device):
        pl.semaphore_signal(barrier, inc=1, device_id=device, device_id_type=MESH)

    at_bottom, at_top, last_peer = row == 0, row == n_rad - 1, me == n - 1

    @pl.when(at_bottom)
    def _():
        everywhere(lambda peer: greet((peer, low)))

    over(me + 1, n, lambda peer: greet((peer, row)))

    @pl.when(jnp.logical_not(at_top))
    def _():
        greet((n - 1, high))

    lane = lax.broadcasted_iota(jnp.int32, (ROWS, LANES), 1)
    line = lax.broadcasted_iota(jnp.int32, (ROWS, LANES), 0)
    box = jnp.broadcast_to(box_ref[...], (ROWS, LANES))
    for f in range(fields):
        gathered[me, f] = box
    loads[0].wait()
    for f in range(fields):
        gathered[me, f, :, 0:row_count] = block_ref[f]
    block = [gathered[me, f] for f in range(fields)]
    to_low = box
    to_high = jnp.zeros((ROWS, LANES), jnp.float32)
    for f in range(fields):
        at = (lane - 4 * f) & (LANES - 1)
        rolled = pltpu.roll(block[f], (LANES - 4 + 4 * f) % LANES, 1)
        to_low = jnp.where((at >= LANES - 4) & (at < LANES - 2), rolled, to_low)
        to_high = jnp.where(at >= LANES - 2, pltpu.roll(block[f], 4 + 4 * f, 1), to_high)
    packs[0] = to_low
    packs[1] = to_high

    greetings = me + jnp.where(at_top, n, 0) + jnp.where(last_peer & (row > 0), n, 0)

    @pl.when(greetings > 0)
    def _():
        pl.semaphore_wait(barrier, greetings)

    def tell(semaphore, device):
        pl.semaphore_signal(semaphore, inc=1, device_id=device, device_id_type=MESH)

    def send(source, target, number, device):
        pltpu.make_async_remote_copy(
            src_ref=source, dst_ref=target,
            send_sem=send_sem.at[number], recv_sem=recv_sem.at[number],
            device_id=device, device_id_type=MESH,
        ).start()

    def send_low():
        everywhere(lambda peer: send(packs.at[0], from_high.at[me], 0, (peer, low)))

    def send_high():
        everywhere(lambda peer: send(packs.at[1], from_low.at[me], 1, (peer, high)))

    def send_block(peer):
        send(gathered.at[me], gathered.at[me], 2, (peer, row))

    def send_block_later(peer):
        pl.semaphore_wait(line_sem.at[peer], 1)
        send_block(peer)

    @pl.when(at_top)
    def _():
        send_high()

    @pl.when(at_top & last_peer)
    def _():
        everywhere(lambda peer: tell(ready_sem.at[0], (peer, high)))

    @pl.when((row > 0) & last_peer)
    def _():
        everywhere(lambda peer: tell(ready_sem.at[1], (peer, low)))
        over(0, n - 1, lambda peer: tell(near_sem, (peer, row)))

    over(0, me, lambda peer: tell(line_sem.at[me], (peer, row)))
    over(0, me, send_block)

    for load in loads[1:]:
        load.wait()
    cells_ref[...] = cells_ref[...] * 256 + fraction_ref[...]
    shifts = jnp.zeros((ROWS, LANES), jnp.int32)
    last = total_rows - LANES

    def loaded(start):
        return jnp.broadcast_to(cells_ref[:, start : start + LANES], (ROWS, LANES))

    for r in range(n_rad):
        start = r * row_count
        from_row = min(start, last)
        here = loaded(from_row)
        if start > from_row:
            here = pltpu.roll(here, LANES - (start - from_row), 1)
        ahead = (start + row_count) % total_rows
        behind = (start - 2) % total_rows
        for first_lane, first_row in ((row_count, ahead), (row_count + 2, behind)):
            begin = min(first_row, last)
            turn = (first_lane - (first_row - begin)) % LANES
            part = loaded(begin)
            part = pltpu.roll(part, turn, 1) if turn else part
            here = jnp.where(lane >= first_lane, part, here)
        shifts = jnp.where(row == r, here, shifts)
    circle = n * strip * 256
    below_box = (lane >= row_count + 2) & (row == 0)
    above_box = (lane >= row_count) & (lane < row_count + 2) & (row == n_rad - 1)
    edge = lane >= row_count

    def coded(total):
        total = jnp.where(total >= circle, total - circle, total)
        first = me * strip - 3 - (total >> 8)
        first = jnp.where(first < 0, first + n * strip, first)
        first = jnp.where(first < 0, first + n * strip, first)
        return first * 256 + (total & 255)

    def code_edges(offset):
        offset = offset.astype(jnp.int32)
        total = shifts + jnp.where(below_box, offset, 0) + jnp.where(above_box, circle - offset, 0)
        packed = jnp.where(edge, coded(total), 0)
        for width in (4, 8, 16):
            packed = packed + pltpu.roll(packed, width, 1)
        edge_ref[...] = packed

    mod_line = line & (strip - 1)
    early = line < strip

    def decoded(value):
        rows = value >> 8
        weight_next = (value & 255).astype(jnp.float32) * (1.0 / 256.0)
        return rows >> (strip.bit_length() - 1), rows & (strip - 1), weight_next

    device, inside, weight_next = decoded(coded(shifts))
    in_low = (lane & 3) >= 2

    def arrived(ref, sem):
        pltpu.make_async_copy(ref, ref, sem).wait()

    over(me + 1, n, send_block_later)

    @pl.when((row > 0) & jnp.logical_not(last_peer))
    def _():
        pl.semaphore_wait(near_sem, 1)

    @pl.when(row > 0)
    def _():
        send_low()

    @pl.when(jnp.logical_not(at_top))
    def _():
        pl.semaphore_wait(ready_sem.at[1], 1)
        send_high()

    @pl.when(at_bottom)
    def _():
        pl.semaphore_wait(ready_sem.at[0], 1)
        send_low()

    others = pl.ds(0, n - 1)

    def chosen(count, where_from, load):
        def choose(e, state):
            values = load(e)
            out = []
            for d in range(3):
                hit = where_from == lax.rem(e + n - d, n)
                out.append([jnp.where(hit, v, h) for v, h in zip(values, state[d])])
            return out

        state = [[jnp.zeros((ROWS, LANES), jnp.float32)] * count for _ in range(3)]
        if n > 16:
            return lax.fori_loop(0, n, choose, state)
        for e in range(n):
            state = choose(e, state)
        return state

    def relocated(three, inside, weight_next):
        total = [None] * planes
        for weight, start in ((1.0 - weight_next, inside + 1), (weight_next, inside)):
            keep = mod_line >= start
            first = jnp.where(keep, three[0], three[1])
            second = jnp.where(keep, three[1], three[2])
            for z in range(planes):
                index = z * strip + ((line + start) & (strip - 1))
                part = weight * jnp.where(early, taken(first, index), taken(second, index))
                total[z] = part if total[z] is None else total[z] + part
        return total

    arrived(gathered.at[others], recv_sem.at[2])

    @pl.when(row != n_rad - 1)
    def _():
        code_edges(gathered[0, 0])

    state = chosen(fields, device, lambda e: [gathered[e, f] for f in range(fields)])
    own = [relocated([s[f] for s in state], inside, weight_next) for f in range(fields)]

    arrived(from_low, recv_sem.at[1])
    arrived(from_high, recv_sem.at[0])

    @pl.when(row == n_rad - 1)
    def _():
        code_edges(pltpu.roll(from_high[0], LANES // 2, 1))

    packed_device, packed_inside, packed_weight = decoded(edge_ref[...])
    state = chosen(1, packed_device, lambda e: [jnp.where(in_low, from_low[e], from_high[e])])
    halo = relocated([s[0] for s in state], packed_inside, packed_weight)
    shifted = [
        [
            jnp.where(edge, pltpu.roll(halo[z], (LANES - 4 * f) % LANES, 1), own[f][z])
            for z in range(planes)
        ]
        for f in range(fields)
    ]

    result = advance(shifted, planes)
    for f in range(fields):
        merged = pltpu.roll(result[0][f], ROWS - 2, 0)
        for z in range(1, planes):
            merged = jnp.where(
                line >= z * strip, pltpu.roll(result[z][f], (z * strip - 2) % ROWS, 0), merged
            )
        out_ref[f] = merged

    arrived(from_high, send_sem.at[0])
    arrived(from_low, send_sem.at[1])
    arrived(gathered.at[others], send_sem.at[2])


def body(plasma, shift_cells, shift_fraction, box_cells, box_fraction):
    fields, planes, strip, row_count = plasma.shape
    assert planes * strip == ROWS and strip + 4 == ROWS and row_count + 4 == LANES
    n, n_rad = lax.axis_size("az"), lax.axis_size("rad")
    total_rows = shift_cells.shape[0]
    block_shape = (fields, ROWS, row_count)
    box = lax.cond(
        (lax.axis_index("az") == 0) & (lax.axis_index("rad") == 0),
        lambda cells, fraction: jnp.broadcast_to(cells * 256 + fraction, (LANES,)).astype(jnp.float32),
        lambda cells, fraction: jnp.zeros((LANES,), jnp.float32),
        box_cells, box_fraction,
    )
    out = pl.pallas_call(
        functools.partial(kernel, n, n_rad, planes),
        out_shape=pltpu.VMEM((fields, ROWS, LANES), jnp.float32),
        in_specs=[pl.BlockSpec(memory_space=pltpu.HBM)] * 3 + [pl.BlockSpec(memory_space=pltpu.VMEM)],
        out_specs=pl.BlockSpec(memory_space=pltpu.VMEM),
        scratch_shapes=[
            pltpu.VMEM(block_shape, jnp.float32),
            pltpu.VMEM((1, total_rows), jnp.int32),
            pltpu.VMEM((1, total_rows), jnp.int32),
            pltpu.VMEM((n, fields, ROWS, LANES), jnp.float32),
            pltpu.VMEM((n, ROWS, LANES), jnp.float32),
            pltpu.VMEM((n, ROWS, LANES), jnp.float32),
            pltpu.VMEM((2, ROWS, LANES), jnp.float32),
            pltpu.SemaphoreType.DMA((3,)),
            pltpu.SemaphoreType.DMA((3,)),
            pltpu.SemaphoreType.DMA((3,)),
            pltpu.SemaphoreType.REGULAR((2,)),
            pltpu.SemaphoreType.REGULAR((n,)),
            pltpu.SemaphoreType.REGULAR,
            pltpu.VMEM((ROWS, LANES), jnp.int32),
        ],
        compiler_params=pltpu.CompilerParams(collective_id=0, has_side_effects=True),
    )(
        plasma.reshape(block_shape),
        shift_cells.reshape(1, total_rows),
        shift_fraction.reshape(1, total_rows),
        box.reshape(1, LANES),
    )
    return out[:, :, :row_count].reshape(plasma.shape)


def solution(mesh):
    placed = (P(None, None, "az", "rad"), P(), P(), P(), P())
    return jax.shard_map(
        body, mesh=mesh, in_specs=placed, out_specs=P(None, None, "az", "rad"), check_vma=False
    )
```

```python
import functools

import jax
import jax.numpy as jnp
from jax import lax
from jax.experimental import pallas as pl
from jax.experimental.pallas import tpu as pltpu
from jax.sharding import PartitionSpec as P

gamma_ratio = 5.0 / 3.0
time_step = 0.05
spin_rate = 1.0
shear_rate = 1.5
MESH = pl.DeviceIdType.MESH
LANES = 128
ROWS = 8
SPARE = 44


def minmod(a, b):
    return jnp.maximum(jnp.minimum(a, b), 0.0) + jnp.minimum(jnp.maximum(a, b), 0.0)


def before(x, axis):
    return pltpu.roll(x, 1, axis)


def after(x, axis):
    return pltpu.roll(x, x.shape[axis] - 1, axis)


def state_terms(primitive, normal_field):
    density, normal_vel, first_vel, second_vel, pressure, first_field, second_field = primitive
    field_sq = normal_field * normal_field + first_field * first_field + second_field * second_field
    total_press = pressure + 0.5 * field_sq
    normal_mom = density * normal_vel
    first_mom = density * first_vel
    second_mom = density * second_vel
    energy = (
        pressure * (1.0 / (gamma_ratio - 1.0))
        + 0.5 * (normal_mom * normal_vel + first_mom * first_vel + second_mom * second_vel)
        + 0.5 * field_sq
    )
    vel_dot_field = normal_vel * normal_field + first_vel * first_field + second_vel * second_field
    conserved = (density, normal_mom, first_mom, second_mom, energy, first_field, second_field)
    fluxes = (
        normal_mom,
        normal_mom * normal_vel + total_press - normal_field * normal_field,
        normal_mom * first_vel - normal_field * first_field,
        normal_mom * second_vel - normal_field * second_field,
        (energy + total_press) * normal_vel - normal_field * vel_dot_field,
        first_field * normal_vel - normal_field * first_vel,
        second_field * normal_vel - normal_field * second_vel,
    )
    stiffness = gamma_ratio * pressure + field_sq
    speed = jnp.abs(normal_vel) + stiffness * lax.rsqrt(stiffness * density)
    return conserved, fluxes, speed


def rusanov(left_state, right_state, normal_field):
    left_cons, left_flux, left_speed = state_terms(left_state, normal_field)
    right_cons, right_flux, right_speed = state_terms(right_state, normal_field)
    half_fastest = 0.5 * jnp.maximum(left_speed, right_speed)
    return [
        0.5 * (lf + rf) - half_fastest * (rc - lc)
        for lf, rf, lc, rc in zip(left_flux, right_flux, left_cons, right_cons)
    ]


def limited(quantity, axis):
    behind, ahead = before(quantity, axis), after(quantity, axis)
    diff = quantity - behind
    half = 0.5 * minmod(diff, ahead - quantity)
    half_behind = 0.5 * minmod(behind - pltpu.roll(quantity, 2, axis), diff)
    return behind + half_behind, quantity - half


def advance(fields, planes):
    rho, vx, vy, vz, p, bx, by, bz = fields
    span = range(planes)
    up = [(z + 1) % planes for z in span]
    down = [(z - 1) % planes for z in span]
    cx = [0.5 * (bx[z] + after(bx[z], 1)) for z in span]
    cy = [0.5 * (by[z] + after(by[z], 0)) for z in span]
    cz = [0.5 * (bz[z] + bz[up[z]]) for z in span]

    def swept(group, axis, normal):
        out = []
        for z in span:
            pairs = [limited(quantity[z], axis) for quantity in group]
            out.append(rusanov([a for a, _ in pairs], [b for _, b in pairs], normal[z]))
        return out

    fx = swept((rho, vx, vy, vz, p, cy, cz), 1, bx)
    fy = swept((rho, vy, vz, vx, p, cz, cx), 0, by)
    group = (rho, vz, vx, vy, p, cx, cy)
    halves = [
        [0.5 * minmod(q[z] - q[down[z]], q[up[z]] - q[z]) for z in span] for q in group
    ]
    fz = [
        rusanov(
            [q[down[z]] + h[down[z]] for q, h in zip(group, halves)],
            [q[z] - h[z] for q, h in zip(group, halves)],
            bz[z],
        )
        for z in span
    ]

    ez = [
        0.25
        * (fy[z][6] + before(fy[z][6], 1) - fx[z][5] - before(fx[z][5], 0))
        for z in span
    ]
    ey = [
        0.25 * (fx[z][6] + fx[down[z]][6] - fz[z][5] - before(fz[z][5], 1)) for z in span
    ]
    ex = [
        0.25 * (fz[z][6] + before(fz[z][6], 0) - fy[z][5] - fy[down[z]][5]) for z in span
    ]
    result = []
    for z in span:
        def total_div(i, j, k):
            return (
                (after(fx[z][i], 1) - fx[z][i])
                + (after(fy[z][j], 0) - fy[z][j])
                + (fz[up[z]][k] - fz[z][k])
            )

        mx, my, mz = rho[z] * vx[z], rho[z] * vy[z], rho[z] * vz[z]
        energy = (
            p[z] * (1.0 / (gamma_ratio - 1.0))
            + 0.5 * (mx * vx[z] + my * vy[z] + mz * vz[z])
            + 0.5 * (cx[z] * cx[z] + cy[z] * cy[z] + cz[z] * cz[z])
        )
        result.append(
            (
                rho[z] - time_step * total_div(0, 0, 0),
                mx - time_step * total_div(1, 3, 2) + (time_step * 2.0 * spin_rate) * my,
                my
                - time_step * total_div(2, 1, 3)
                - (time_step * (2.0 - shear_rate) * spin_rate) * mx,
                mz - time_step * total_div(3, 2, 1),
                energy - time_step * total_div(4, 4, 4),
                bx[z] - time_step * (after(ez[z], 0) - ez[z] - (ey[up[z]] - ey[z])),
                by[z] - time_step * (ex[up[z]] - ex[z] - (after(ez[z], 1) - ez[z])),
                bz[z] - time_step * (after(ey[z], 1) - ey[z] - (after(ex[z], 0) - ex[z])),
            )
        )
    return result


def taken(x, index):
    return jnp.take_along_axis(x, index, axis=0, mode="promise_in_bounds")


def kernel(
    n, n_rad, planes, plasma_any, cells_any, fraction_any, box_ref, out_ref,
    block_ref, cells_ref, fraction_ref,
    gathered, from_low, from_high, packs, load_sem, send_sem, recv_sem,
    ready_sem, line_sem, near_sem, edge_ref,
):
    fields = block_ref.shape[0]
    strip = ROWS // planes
    row_count = plasma_any.shape[2]
    total_rows = cells_ref.shape[1]
    me, row = lax.axis_index("az"), lax.axis_index("rad")
    low, high = lax.rem(row + n_rad - 1, n_rad), lax.rem(row + 1, n_rad)

    def over(first, last, body):
        lax.fori_loop(first, last, lambda peer, _: (body(peer), 0)[1], 0)

    def everywhere(body):
        if n <= 16:
            for peer in range(n):
                body(peer)
        else:
            over(0, n, body)

    loads = [
        pltpu.make_async_copy(source, target, load_sem.at[number])
        for number, (source, target) in enumerate(
            (
                (plasma_any, block_ref),
                (cells_any, cells_ref),
                (fraction_any, fraction_ref),
            )
        )
    ]
    for load in loads:
        load.start()

    barrier = pltpu.get_barrier_semaphore()

    def greet(device):
        pl.semaphore_signal(barrier, inc=1, device_id=device, device_id_type=MESH)

    at_bottom, at_top, last_peer = row == 0, row == n_rad - 1, me == n - 1

    @pl.when(at_bottom)
    def _():
        everywhere(lambda peer: greet((peer, low)))

    over(me + 1, n, lambda peer: greet((peer, row)))

    @pl.when(jnp.logical_not(at_top))
    def _():
        greet((n - 1, high))

    lane = lax.broadcasted_iota(jnp.int32, (ROWS, LANES), 1)
    line = lax.broadcasted_iota(jnp.int32, (ROWS, LANES), 0)
    box = jnp.broadcast_to(box_ref[...], (ROWS, LANES))
    for f in range(fields):
        gathered[me, f] = box
    loads[0].wait()
    for f in range(fields):
        gathered[me, f, :, 0:row_count] = block_ref[f]
    apart = LANES // planes
    places = [(f, z, 4 * f + apart * z) for z in range(planes) for f in range(fields)]
    strip_lane = lane[0:strip]
    block = [gathered[me, f, z * strip : (z + 1) * strip] for f, z, _ in places]
    to_high = jnp.zeros((strip, LANES), jnp.float32)
    for source, (f, z, place) in zip(block, places):
        at = (strip_lane - place) & (LANES - 1)
        to_high = jnp.where(at >= LANES - 2, pltpu.roll(source, (4 + place) % LANES, 1), to_high)
    packs[1] = to_high

    greetings = me + jnp.where(at_top, n, 0) + jnp.where(last_peer & (row > 0), n, 0)

    @pl.when(greetings > 0)
    def _():
        pl.semaphore_wait(barrier, greetings)

    def tell(semaphore, device):
        pl.semaphore_signal(semaphore, inc=1, device_id=device, device_id_type=MESH)

    def send(source, target, number, device):
        pltpu.make_async_remote_copy(
            src_ref=source, dst_ref=target,
            send_sem=send_sem.at[number], recv_sem=recv_sem.at[number],
            device_id=device, device_id_type=MESH,
        ).start()

    def send_low():
        everywhere(lambda peer: send(packs.at[0], from_high.at[me], 0, (peer, low)))

    def send_high():
        everywhere(lambda peer: send(packs.at[1], from_low.at[me], 1, (peer, high)))

    def send_block(peer):
        send(gathered.at[me], gathered.at[me], 2, (peer, row))

    def send_block_later(peer):
        pl.semaphore_wait(line_sem.at[peer], 1)
        send_block(peer)

    @pl.when(at_top)
    def _():
        send_high()

    @pl.when(at_top & last_peer)
    def _():
        everywhere(lambda peer: tell(ready_sem.at[0], (peer, high)))

    @pl.when((row > 0) & last_peer)
    def _():
        everywhere(lambda peer: tell(ready_sem.at[1], (peer, low)))
        over(0, n - 1, lambda peer: tell(near_sem, (peer, row)))

    to_low = box[0:strip]
    for source, (f, z, place) in zip(block, places):
        at = (strip_lane - place) & (LANES - 1)
        rolled = pltpu.roll(source, (LANES - 4 + place) % LANES, 1)
        to_low = jnp.where((at >= LANES - 4) & (at < LANES - 2), rolled, to_low)
    packs[0] = to_low

    over(0, me, lambda peer: tell(line_sem.at[me], (peer, row)))
    over(0, me, send_block)

    for load in loads[1:]:
        load.wait()
    cells_ref[...] = cells_ref[...] * 256 + fraction_ref[...]
    shifts = jnp.zeros((ROWS, LANES), jnp.int32)
    last = total_rows - LANES

    def loaded(start):
        return jnp.broadcast_to(cells_ref[:, start : start + LANES], (ROWS, LANES))

    for r in range(n_rad):
        start = r * row_count
        from_row = min(start, last)
        here = loaded(from_row)
        if start > from_row:
            here = pltpu.roll(here, LANES - (start - from_row), 1)
        ahead = (start + row_count) % total_rows
        behind = (start - 2) % total_rows
        for first_lane, first_row in ((row_count, ahead), (row_count + 2, behind)):
            begin = min(first_row, last)
            turn = (first_lane - (first_row - begin)) % LANES
            part = loaded(begin)
            part = pltpu.roll(part, turn, 1) if turn else part
            here = jnp.where(lane >= first_lane, part, here)
        shifts = jnp.where(row == r, here, shifts)
    circle = n * strip * 256
    below_box = (lane >= row_count + 2) & (row == 0)
    above_box = (lane >= row_count) & (lane < row_count + 2) & (row == n_rad - 1)
    edge = lane >= row_count

    def coded(total):
        total = jnp.where(total >= circle, total - circle, total)
        first = me * strip - 3 - (total >> 8)
        first = jnp.where(first < 0, first + n * strip, first)
        first = jnp.where(first < 0, first + n * strip, first)
        return first * 256 + (total & 255)

    def code_edges(offset):
        offset = offset.astype(jnp.int32)
        total = shifts + jnp.where(below_box, offset, 0) + jnp.where(above_box, circle - offset, 0)
        packed = jnp.where(edge, coded(total), 0)
        for width in (4, 8, 16, apart):
            packed = packed + pltpu.roll(packed, width, 1)
        edge_ref[...] = packed

    mod_line = line & (strip - 1)
    early = line < strip

    def decoded(value):
        rows = value >> 8
        weight_next = (value & 255).astype(jnp.float32) * (1.0 / 256.0)
        return rows >> (strip.bit_length() - 1), rows & (strip - 1), weight_next

    device, inside, weight_next = decoded(coded(shifts))
    in_low = (strip_lane & 3) >= 2

    def arrived(ref, sem):
        pltpu.make_async_copy(ref, ref, sem).wait()

    over(me + 1, n, send_block_later)

    @pl.when((row > 0) & jnp.logical_not(last_peer))
    def _():
        pl.semaphore_wait(near_sem, 1)

    @pl.when(row > 0)
    def _():
        send_low()

    @pl.when(jnp.logical_not(at_top))
    def _():
        pl.semaphore_wait(ready_sem.at[1], 1)
        send_high()

    @pl.when(at_bottom)
    def _():
        pl.semaphore_wait(ready_sem.at[0], 1)
        send_low()

    others = pl.ds(0, n - 1)

    def chosen(count, where_from, load):
        def choose(e, state):
            values = load(e)
            out = []
            for d in range(3):
                hit = where_from == lax.rem(e + n - d, n)
                out.append([jnp.where(hit, v, h) for v, h in zip(values, state[d])])
            return out

        state = [[jnp.zeros(where_from.shape, jnp.float32)] * count for _ in range(3)]
        if n > 16:
            return lax.fori_loop(0, n, choose, state)
        for e in range(n):
            state = choose(e, state)
        return state

    def relocated(three, inside, weight_next):
        total = [None] * planes
        for weight, start in ((1.0 - weight_next, inside + 1), (weight_next, inside)):
            keep = mod_line >= start
            first = jnp.where(keep, three[0], three[1])
            second = jnp.where(keep, three[1], three[2])
            for z in range(planes):
                index = z * strip + ((line + start) & (strip - 1))
                part = weight * jnp.where(early, taken(first, index), taken(second, index))
                total[z] = part if total[z] is None else total[z] + part
        return total

    arrived(gathered.at[others], recv_sem.at[2])

    @pl.when(row != n_rad - 1)
    def _():
        code_edges(gathered[0, 0])

    state = chosen(fields, device, lambda e: [gathered[e, f] for f in range(fields)])
    own = [relocated([s[f] for s in state], inside, weight_next) for f in range(fields)]

    arrived(from_low, recv_sem.at[1])
    arrived(from_high, recv_sem.at[0])

    @pl.when(row == n_rad - 1)
    def _():
        spare = jnp.broadcast_to(from_high[0, 0:1], (ROWS, LANES))
        code_edges(pltpu.roll(spare, LANES - SPARE - 4, 1))

    packed_device, packed_inside, packed_weight = decoded(edge_ref[...])
    state = chosen(
        1, packed_device[0:strip], lambda e: [jnp.where(in_low, from_low[e], from_high[e])]
    )
    three = [jnp.concatenate([s[0]] * planes, axis=0) for s in state]
    halo = 0.0
    for weight, start in (
        (1.0 - packed_weight, packed_inside + 1), (packed_weight, packed_inside)
    ):
        keep = mod_line >= start
        index = (line + start) & (strip - 1)
        first = taken(jnp.where(keep, three[0], three[1]), index)
        second = taken(jnp.where(keep, three[1], three[2]), index)
        halo = halo + weight * jnp.where(early, first, second)
    shifted = [
        [
            jnp.where(edge, pltpu.roll(halo, (2 * LANES - 4 * f - apart * z) % LANES, 1), own[f][z])
            for z in range(planes)
        ]
        for f in range(fields)
    ]

    result = advance(shifted, planes)
    for f in range(fields):
        for z in range(planes):
            out_ref[f, z * strip : (z + 1) * strip] = result[z][f][2 : 2 + strip]

    arrived(from_high, send_sem.at[0])
    arrived(from_low, send_sem.at[1])
    arrived(gathered.at[others], send_sem.at[2])


def body(plasma, shift_cells, shift_fraction, box_cells, box_fraction):
    fields, planes, strip, row_count = plasma.shape
    assert planes * strip == ROWS and strip + 4 == ROWS and row_count + 4 == LANES
    assert 4 * fields - 4 <= SPARE <= LANES // planes - 8
    n, n_rad = lax.axis_size("az"), lax.axis_size("rad")
    total_rows = shift_cells.shape[0]
    block_shape = (fields, ROWS, row_count)
    box = lax.cond(
        (lax.axis_index("az") == 0) & (lax.axis_index("rad") == 0),
        lambda cells, fraction: jnp.broadcast_to(cells * 256 + fraction, (LANES,)).astype(jnp.float32),
        lambda cells, fraction: jnp.zeros((LANES,), jnp.float32),
        box_cells, box_fraction,
    )
    out = pl.pallas_call(
        functools.partial(kernel, n, n_rad, planes),
        out_shape=pltpu.VMEM((fields, ROWS, LANES), jnp.float32),
        in_specs=[pl.BlockSpec(memory_space=pltpu.HBM)] * 3 + [pl.BlockSpec(memory_space=pltpu.VMEM)],
        out_specs=pl.BlockSpec(memory_space=pltpu.VMEM),
        scratch_shapes=[
            pltpu.VMEM(block_shape, jnp.float32),
            pltpu.VMEM((1, total_rows), jnp.int32),
            pltpu.VMEM((1, total_rows), jnp.int32),
            pltpu.VMEM((n, fields, ROWS, LANES), jnp.float32),
            pltpu.VMEM((n, strip, LANES), jnp.float32),
            pltpu.VMEM((n, strip, LANES), jnp.float32),
            pltpu.VMEM((2, strip, LANES), jnp.float32),
            pltpu.SemaphoreType.DMA((3,)),
            pltpu.SemaphoreType.DMA((3,)),
            pltpu.SemaphoreType.DMA((3,)),
            pltpu.SemaphoreType.REGULAR((2,)),
            pltpu.SemaphoreType.REGULAR((n,)),
            pltpu.SemaphoreType.REGULAR,
            pltpu.VMEM((ROWS, LANES), jnp.int32),
        ],
        compiler_params=pltpu.CompilerParams(collective_id=0, has_side_effects=True),
    )(
        plasma.reshape(block_shape),
        shift_cells.reshape(1, total_rows),
        shift_fraction.reshape(1, total_rows),
        box.reshape(1, LANES),
    )
    return out[:, :, :row_count].reshape(plasma.shape)


def solution(mesh):
    placed = (P(None, None, "az", "rad"), P(), P(), P(), P())
    return jax.shard_map(
        body, mesh=mesh, in_specs=placed, out_specs=P(None, None, "az", "rad"), check_vma=False
    )
```

```python
import functools

import jax
import jax.numpy as jnp
from jax import lax
from jax.experimental import pallas as pl
from jax.experimental.pallas import tpu as pltpu
from jax.sharding import PartitionSpec as P

gamma_ratio = 5.0 / 3.0
time_step = 0.05
spin_rate = 1.0
shear_rate = 1.5
flux_step = 0.5 * time_step
edge_step = 0.125 * time_step
MESH = pl.DeviceIdType.MESH
LANES = 128
ROWS = 8
SPARE = 44


def minmod(a, b):
    return jnp.maximum(jnp.minimum(a, b), 0.0) + jnp.minimum(jnp.maximum(a, b), 0.0)


def before(x, axis):
    return pltpu.roll(x, 1, axis)


def after(x, axis):
    return pltpu.roll(x, x.shape[axis] - 1, axis)


def state_terms(primitive, normal_field):
    density, normal_vel, first_vel, second_vel, pressure, first_field, second_field = primitive
    field_sq = normal_field * normal_field + first_field * first_field + second_field * second_field
    total_press = pressure + 0.5 * field_sq
    normal_mom = density * normal_vel
    first_mom = density * first_vel
    second_mom = density * second_vel
    energy = (
        pressure * (1.0 / (gamma_ratio - 1.0))
        + 0.5 * (normal_mom * normal_vel + first_mom * first_vel + second_mom * second_vel)
        + 0.5 * field_sq
    )
    vel_dot_field = normal_vel * normal_field + first_vel * first_field + second_vel * second_field
    conserved = (density, normal_mom, first_mom, second_mom, energy, first_field, second_field)
    fluxes = (
        normal_mom,
        normal_mom * normal_vel + total_press - normal_field * normal_field,
        normal_mom * first_vel - normal_field * first_field,
        normal_mom * second_vel - normal_field * second_field,
        (energy + total_press) * normal_vel - normal_field * vel_dot_field,
        first_field * normal_vel - normal_field * first_vel,
        second_field * normal_vel - normal_field * second_vel,
    )
    stiffness = gamma_ratio * pressure + field_sq
    speed = jnp.abs(normal_vel) + stiffness * lax.rsqrt(stiffness * density)
    return conserved, fluxes, speed


def rusanov(left_state, right_state, normal_field):
    left_cons, left_flux, left_speed = state_terms(left_state, normal_field)
    right_cons, right_flux, right_speed = state_terms(right_state, normal_field)
    fastest = jnp.maximum(left_speed, right_speed)
    return [
        (lf + rf) - fastest * (rc - lc)
        for lf, rf, lc, rc in zip(left_flux, right_flux, left_cons, right_cons)
    ]


def limited(quantity, axis):
    behind, ahead = before(quantity, axis), after(quantity, axis)
    diff = quantity - behind
    half = 0.5 * minmod(diff, ahead - quantity)
    half_behind = 0.5 * minmod(behind - pltpu.roll(quantity, 2, axis), diff)
    return behind + half_behind, quantity - half


def advance(fields, planes):
    rho, vx, vy, vz, p, bx, by, bz = fields
    span = range(planes)
    up = [(z + 1) % planes for z in span]
    down = [(z - 1) % planes for z in span]
    cx = [0.5 * (bx[z] + after(bx[z], 1)) for z in span]
    cy = [0.5 * (by[z] + after(by[z], 0)) for z in span]
    cz = [0.5 * (bz[z] + bz[up[z]]) for z in span]

    def swept(group, axis, normal):
        out = []
        for z in span:
            pairs = [limited(quantity[z], axis) for quantity in group]
            out.append(rusanov([a for a, _ in pairs], [b for _, b in pairs], normal[z]))
        return out

    fx = swept((rho, vx, vy, vz, p, cy, cz), 1, bx)
    fy = swept((rho, vy, vz, vx, p, cz, cx), 0, by)
    group = (rho, vz, vx, vy, p, cx, cy)
    halves = [
        [0.5 * minmod(q[z] - q[down[z]], q[up[z]] - q[z]) for z in span] for q in group
    ]
    fz = [
        rusanov(
            [q[down[z]] + h[down[z]] for q, h in zip(group, halves)],
            [q[z] - h[z] for q, h in zip(group, halves)],
            bz[z],
        )
        for z in span
    ]

    ez = [
        (fy[z][6] + before(fy[z][6], 1) - fx[z][5] - before(fx[z][5], 0))
        for z in span
    ]
    ey = [
        (fx[z][6] + fx[down[z]][6] - fz[z][5] - before(fz[z][5], 1)) for z in span
    ]
    ex = [
        (fz[z][6] + before(fz[z][6], 0) - fy[z][5] - fy[down[z]][5]) for z in span
    ]
    result = []
    for z in span:
        def total_div(i, j, k):
            return (
                (after(fx[z][i], 1) - fx[z][i])
                + (after(fy[z][j], 0) - fy[z][j])
                + (fz[up[z]][k] - fz[z][k])
            )

        mx, my, mz = rho[z] * vx[z], rho[z] * vy[z], rho[z] * vz[z]
        energy = (
            p[z] * (1.0 / (gamma_ratio - 1.0))
            + 0.5 * (mx * vx[z] + my * vy[z] + mz * vz[z])
            + 0.5 * (cx[z] * cx[z] + cy[z] * cy[z] + cz[z] * cz[z])
        )
        result.append(
            (
                rho[z] - flux_step * total_div(0, 0, 0),
                mx - flux_step * total_div(1, 3, 2) + (time_step * 2.0 * spin_rate) * my,
                my
                - flux_step * total_div(2, 1, 3)
                - (time_step * (2.0 - shear_rate) * spin_rate) * mx,
                mz - flux_step * total_div(3, 2, 1),
                energy - flux_step * total_div(4, 4, 4),
                bx[z] - edge_step * (after(ez[z], 0) - ez[z] - (ey[up[z]] - ey[z])),
                by[z] - edge_step * (ex[up[z]] - ex[z] - (after(ez[z], 1) - ez[z])),
                bz[z] - edge_step * (after(ey[z], 1) - ey[z] - (after(ex[z], 0) - ex[z])),
            )
        )
    return result


def taken(x, index):
    return jnp.take_along_axis(x, index, axis=0, mode="promise_in_bounds")


def kernel(
    n, n_rad, planes, plasma_any, cells_any, fraction_any, box_ref, out_ref,
    block_ref, cells_ref, fraction_ref,
    gathered, from_low, from_high, packs, load_sem, send_sem, recv_sem,
    ready_sem, line_sem, near_sem, edge_ref, edge_weight_ref,
):
    fields = block_ref.shape[0]
    strip = ROWS // planes
    row_count = plasma_any.shape[2]
    total_rows = cells_ref.shape[1]
    me, row = lax.axis_index("az"), lax.axis_index("rad")
    low, high = lax.rem(row + n_rad - 1, n_rad), lax.rem(row + 1, n_rad)

    def over(first, last, body):
        lax.fori_loop(first, last, lambda peer, _: (body(peer), 0)[1], 0)

    def everywhere(body):
        if n <= 16:
            for peer in range(n):
                body(peer)
        else:
            over(0, n, body)

    loads = [
        pltpu.make_async_copy(source, target, load_sem.at[number])
        for number, (source, target) in enumerate(
            (
                (plasma_any, block_ref),
                (cells_any, cells_ref),
                (fraction_any, fraction_ref),
            )
        )
    ]
    for load in loads:
        load.start()

    barrier = pltpu.get_barrier_semaphore()

    def greet(device):
        pl.semaphore_signal(barrier, inc=1, device_id=device, device_id_type=MESH)

    at_bottom, at_top, last_peer = row == 0, row == n_rad - 1, me == n - 1

    @pl.when(at_bottom)
    def _():
        everywhere(lambda peer: greet((peer, low)))

    over(me + 1, n, lambda peer: greet((peer, row)))

    @pl.when(jnp.logical_not(at_top))
    def _():
        greet((n - 1, high))

    lane = lax.broadcasted_iota(jnp.int32, (ROWS, LANES), 1)
    line = lax.broadcasted_iota(jnp.int32, (ROWS, LANES), 0)
    box = jnp.broadcast_to(box_ref[...], (ROWS, LANES))
    for f in range(fields):
        gathered[me, f] = box
    loads[0].wait()
    for f in range(fields):
        gathered[me, f, :, 0:row_count] = block_ref[f]
    apart = LANES // planes
    places = [(f, z, 4 * f + apart * z) for z in range(planes) for f in range(fields)]
    strip_lane = lane[0:strip]
    block = [gathered[me, f, z * strip : (z + 1) * strip] for f, z, _ in places]
    to_high = jnp.zeros((strip, LANES), jnp.float32)
    for source, (f, z, place) in zip(block, places):
        at = (strip_lane - place) & (LANES - 1)
        to_high = jnp.where(at >= LANES - 2, pltpu.roll(source, (4 + place) % LANES, 1), to_high)
    packs[1] = to_high

    greetings = me + jnp.where(at_top, n, 0) + jnp.where(last_peer & (row > 0), n, 0)

    @pl.when(greetings > 0)
    def _():
        pl.semaphore_wait(barrier, greetings)

    def tell(semaphore, device):
        pl.semaphore_signal(semaphore, inc=1, device_id=device, device_id_type=MESH)

    def send(source, target, number, device):
        pltpu.make_async_remote_copy(
            src_ref=source, dst_ref=target,
            send_sem=send_sem.at[number], recv_sem=recv_sem.at[number],
            device_id=device, device_id_type=MESH,
        ).start()

    def send_low():
        everywhere(lambda peer: send(packs.at[0], from_high.at[me], 0, (peer, low)))

    def send_high():
        everywhere(lambda peer: send(packs.at[1], from_low.at[me], 1, (peer, high)))

    def send_block(peer):
        send(gathered.at[me], gathered.at[me], 2, (peer, row))

    def send_block_later(peer):
        pl.semaphore_wait(line_sem.at[peer], 1)
        send_block(peer)

    @pl.when(at_top)
    def _():
        send_high()

    @pl.when(at_top & last_peer)
    def _():
        everywhere(lambda peer: tell(ready_sem.at[0], (peer, high)))

    @pl.when((row > 0) & last_peer)
    def _():
        everywhere(lambda peer: tell(ready_sem.at[1], (peer, low)))
        over(0, n - 1, lambda peer: tell(near_sem, (peer, row)))

    to_low = box[0:strip]
    for source, (f, z, place) in zip(block, places):
        at = (strip_lane - place) & (LANES - 1)
        rolled = pltpu.roll(source, (LANES - 4 + place) % LANES, 1)
        to_low = jnp.where((at >= LANES - 4) & (at < LANES - 2), rolled, to_low)
    packs[0] = to_low

    over(0, me, lambda peer: tell(line_sem.at[me], (peer, row)))
    over(0, me, send_block)

    for load in loads[1:]:
        load.wait()
    cells_ref[...] = cells_ref[...] * 256 + fraction_ref[...]
    shifts = jnp.zeros((ROWS, LANES), jnp.int32)
    last = total_rows - LANES

    def loaded(start):
        return jnp.broadcast_to(cells_ref[:, start : start + LANES], (ROWS, LANES))

    for r in range(n_rad):
        start = r * row_count
        from_row = min(start, last)
        here = loaded(from_row)
        if start > from_row:
            here = pltpu.roll(here, LANES - (start - from_row), 1)
        ahead = (start + row_count) % total_rows
        behind = (start - 2) % total_rows
        for first_lane, first_row in ((row_count, ahead), (row_count + 2, behind)):
            begin = min(first_row, last)
            turn = (first_lane - (first_row - begin)) % LANES
            part = loaded(begin)
            part = pltpu.roll(part, turn, 1) if turn else part
            here = jnp.where(lane >= first_lane, part, here)
        shifts = jnp.where(row == r, here, shifts)
    circle = n * strip * 256
    below_box = (lane >= row_count + 2) & (row == 0)
    above_box = (lane >= row_count) & (lane < row_count + 2) & (row == n_rad - 1)
    edge = lane >= row_count

    def coded(total):
        total = jnp.where(total >= circle, total - circle, total)
        first = me * strip - 3 - (total >> 8)
        first = jnp.where(first < 0, first + n * strip, first)
        first = jnp.where(first < 0, first + n * strip, first)
        return first * 256 + (total & 255)

    def code_edges(offset):
        offset = offset.astype(jnp.int32)
        total = shifts + jnp.where(below_box, offset, 0) + jnp.where(above_box, circle - offset, 0)
        packed = jnp.where(edge, coded(total), 0)
        for width in (4, 8, 16, apart):
            packed = packed + pltpu.roll(packed, width, 1)
        rows, inner, next_weight = decoded(packed)
        edge_ref[0] = rows
        edge_ref[1] = inner
        edge_weight_ref[...] = next_weight

    mod_line = line & (strip - 1)
    early = line < strip

    def decoded(value):
        rows = value >> 8
        weight_next = (value & 255).astype(jnp.float32) * (1.0 / 256.0)
        return rows >> (strip.bit_length() - 1), rows & (strip - 1), weight_next

    device, inside, weight_next = decoded(coded(shifts))
    in_low = (strip_lane & 3) >= 2

    def arrived(ref, sem):
        pltpu.make_async_copy(ref, ref, sem).wait()

    over(me + 1, n, send_block_later)

    @pl.when((row > 0) & jnp.logical_not(last_peer))
    def _():
        pl.semaphore_wait(near_sem, 1)

    @pl.when(row > 0)
    def _():
        send_low()

    @pl.when(jnp.logical_not(at_top))
    def _():
        pl.semaphore_wait(ready_sem.at[1], 1)
        send_high()

    @pl.when(at_bottom)
    def _():
        pl.semaphore_wait(ready_sem.at[0], 1)
        send_low()

    others = pl.ds(0, n - 1)

    def chosen(count, where_from, load):
        def choose(e, state):
            values = load(e)
            out = []
            for d in range(3):
                hit = where_from == lax.rem(e + n - d, n)
                out.append([jnp.where(hit, v, h) for v, h in zip(values, state[d])])
            return out

        state = [[jnp.zeros(where_from.shape, jnp.float32)] * count for _ in range(3)]
        if n > 16:
            return lax.fori_loop(0, n, choose, state)
        for e in range(n):
            state = choose(e, state)
        return state

    def relocated(three, inside, weight_next):
        total = [None] * planes
        for weight, start in ((1.0 - weight_next, inside + 1), (weight_next, inside)):
            keep = mod_line >= start
            first = jnp.where(keep, three[0], three[1])
            second = jnp.where(keep, three[1], three[2])
            for z in range(planes):
                index = z * strip + ((line + start) & (strip - 1))
                part = weight * jnp.where(early, taken(first, index), taken(second, index))
                total[z] = part if total[z] is None else total[z] + part
        return total

    arrived(gathered.at[others], recv_sem.at[2])

    @pl.when(row != n_rad - 1)
    def _():
        code_edges(gathered[0, 0])

    state = chosen(fields, device, lambda e: [gathered[e, f] for f in range(fields)])
    own = [relocated([s[f] for s in state], inside, weight_next) for f in range(fields)]

    arrived(from_low, recv_sem.at[1])
    arrived(from_high, recv_sem.at[0])

    @pl.when(row == n_rad - 1)
    def _():
        spare = jnp.broadcast_to(from_high[0, 0:1], (ROWS, LANES))
        code_edges(pltpu.roll(spare, LANES - SPARE - 4, 1))

    packed_device, packed_inside, packed_weight = edge_ref[0], edge_ref[1], edge_weight_ref[...]
    state = chosen(
        1, packed_device[0:strip], lambda e: [jnp.where(in_low, from_low[e], from_high[e])]
    )
    three = [jnp.concatenate([s[0]] * planes, axis=0) for s in state]
    halo = 0.0
    for weight, start in (
        (1.0 - packed_weight, packed_inside + 1), (packed_weight, packed_inside)
    ):
        keep = mod_line >= start
        index = (line + start) & (strip - 1)
        first = taken(jnp.where(keep, three[0], three[1]), index)
        second = taken(jnp.where(keep, three[1], three[2]), index)
        halo = halo + weight * jnp.where(early, first, second)
    shifted = [
        [
            jnp.where(edge, pltpu.roll(halo, (2 * LANES - 4 * f - apart * z) % LANES, 1), own[f][z])
            for z in range(planes)
        ]
        for f in range(fields)
    ]

    result = advance(shifted, planes)
    for f in range(fields):
        for z in range(planes):
            out_ref[f, z * strip : (z + 1) * strip] = result[z][f][2 : 2 + strip]

    arrived(from_high, send_sem.at[0])
    arrived(from_low, send_sem.at[1])
    arrived(gathered.at[others], send_sem.at[2])


def body(plasma, shift_cells, shift_fraction, box_cells, box_fraction):
    fields, planes, strip, row_count = plasma.shape
    assert planes * strip == ROWS and strip + 4 == ROWS and row_count + 4 == LANES
    assert 4 * fields - 4 <= SPARE <= LANES // planes - 8
    n, n_rad = lax.axis_size("az"), lax.axis_size("rad")
    total_rows = shift_cells.shape[0]
    block_shape = (fields, ROWS, row_count)
    box = lax.cond(
        (lax.axis_index("az") == 0) & (lax.axis_index("rad") == 0),
        lambda cells, fraction: jnp.broadcast_to(cells * 256 + fraction, (LANES,)).astype(jnp.float32),
        lambda cells, fraction: jnp.zeros((LANES,), jnp.float32),
        box_cells, box_fraction,
    )
    out = pl.pallas_call(
        functools.partial(kernel, n, n_rad, planes),
        out_shape=pltpu.VMEM((fields, ROWS, LANES), jnp.float32),
        in_specs=[pl.BlockSpec(memory_space=pltpu.HBM)] * 3 + [pl.BlockSpec(memory_space=pltpu.VMEM)],
        out_specs=pl.BlockSpec(memory_space=pltpu.VMEM),
        scratch_shapes=[
            pltpu.VMEM(block_shape, jnp.float32),
            pltpu.VMEM((1, total_rows), jnp.int32),
            pltpu.VMEM((1, total_rows), jnp.int32),
            pltpu.VMEM((n, fields, ROWS, LANES), jnp.float32),
            pltpu.VMEM((n, strip, LANES), jnp.float32),
            pltpu.VMEM((n, strip, LANES), jnp.float32),
            pltpu.VMEM((2, strip, LANES), jnp.float32),
            pltpu.SemaphoreType.DMA((3,)),
            pltpu.SemaphoreType.DMA((3,)),
            pltpu.SemaphoreType.DMA((3,)),
            pltpu.SemaphoreType.REGULAR((2,)),
            pltpu.SemaphoreType.REGULAR((n,)),
            pltpu.SemaphoreType.REGULAR,
            pltpu.VMEM((2, ROWS, LANES), jnp.int32),
            pltpu.VMEM((ROWS, LANES), jnp.float32),
        ],
        compiler_params=pltpu.CompilerParams(collective_id=0, has_side_effects=True),
    )(
        plasma.reshape(block_shape),
        shift_cells.reshape(1, total_rows),
        shift_fraction.reshape(1, total_rows),
        box.reshape(1, LANES),
    )
    return out[:, :, :row_count].reshape(plasma.shape)


def solution(mesh):
    placed = (P(None, None, "az", "rad"), P(), P(), P(), P())
    return jax.shard_map(
        body, mesh=mesh, in_specs=placed, out_specs=P(None, None, "az", "rad"), check_vma=False
    )
```

```python
import functools

import jax
import jax.numpy as jnp
from jax import lax
from jax.experimental import pallas as pl
from jax.experimental.pallas import tpu as pltpu
from jax.sharding import PartitionSpec as P

gamma_ratio = 5.0 / 3.0
time_step = 0.05
spin_rate = 1.0
shear_rate = 1.5
flux_step = 0.5 * time_step
edge_step = 0.125 * time_step
MESH = pl.DeviceIdType.MESH
LANES = 128
ROWS = 8
SPARE = 44


def minmod(a, b):
    return jnp.maximum(jnp.minimum(a, b), 0.0) + jnp.minimum(jnp.maximum(a, b), 0.0)


def before(x, axis):
    return pltpu.roll(x, 1, axis)


def after(x, axis):
    return pltpu.roll(x, x.shape[axis] - 1, axis)


def state_terms(primitive, normal_field):
    density, normal_vel, first_vel, second_vel, pressure, first_field, second_field = primitive
    field_sq = normal_field * normal_field + first_field * first_field + second_field * second_field
    total_press = pressure + 0.5 * field_sq
    normal_mom = density * normal_vel
    first_mom = density * first_vel
    second_mom = density * second_vel
    energy = (
        pressure * (1.0 / (gamma_ratio - 1.0))
        + 0.5 * (normal_mom * normal_vel + first_mom * first_vel + second_mom * second_vel)
        + 0.5 * field_sq
    )
    vel_dot_field = normal_vel * normal_field + first_vel * first_field + second_vel * second_field
    conserved = (density, normal_mom, first_mom, second_mom, energy, first_field, second_field)
    fluxes = (
        normal_mom,
        normal_mom * normal_vel + total_press - normal_field * normal_field,
        normal_mom * first_vel - normal_field * first_field,
        normal_mom * second_vel - normal_field * second_field,
        (energy + total_press) * normal_vel - normal_field * vel_dot_field,
        first_field * normal_vel - normal_field * first_vel,
        second_field * normal_vel - normal_field * second_vel,
    )
    stiffness = gamma_ratio * pressure + field_sq
    speed = jnp.abs(normal_vel) + stiffness * lax.rsqrt(stiffness * density)
    return conserved, fluxes, speed


def rusanov(left_state, right_state, normal_field):
    left_cons, left_flux, left_speed = state_terms(left_state, normal_field)
    right_cons, right_flux, right_speed = state_terms(right_state, normal_field)
    fastest = jnp.maximum(left_speed, right_speed)
    return [
        (lf + rf) - fastest * (rc - lc)
        for lf, rf, lc, rc in zip(left_flux, right_flux, left_cons, right_cons)
    ]


def limited(quantity, axis):
    behind, ahead = before(quantity, axis), after(quantity, axis)
    diff = quantity - behind
    half = 0.5 * minmod(diff, ahead - quantity)
    half_behind = 0.5 * minmod(behind - pltpu.roll(quantity, 2, axis), diff)
    return behind + half_behind, quantity - half


def advance(fields, planes):
    rho, vx, vy, vz, p, bx, by, bz = fields
    span = range(planes)
    up = [(z + 1) % planes for z in span]
    down = [(z - 1) % planes for z in span]
    cx = [0.5 * (bx[z] + after(bx[z], 1)) for z in span]
    cy = [0.5 * (by[z] + after(by[z], 0)) for z in span]
    cz = [0.5 * (bz[z] + bz[up[z]]) for z in span]

    def swept(group, axis, normal):
        out = []
        for z in span:
            pairs = [limited(quantity[z], axis) for quantity in group]
            out.append(rusanov([a for a, _ in pairs], [b for _, b in pairs], normal[z]))
        return out

    fx = swept((rho, vx, vy, vz, p, cy, cz), 1, bx)
    fy = swept((rho, vy, vz, vx, p, cz, cx), 0, by)
    group = (rho, vz, vx, vy, p, cx, cy)
    halves = [
        [0.5 * minmod(q[z] - q[down[z]], q[up[z]] - q[z]) for z in span] for q in group
    ]
    fz = [
        rusanov(
            [q[down[z]] + h[down[z]] for q, h in zip(group, halves)],
            [q[z] - h[z] for q, h in zip(group, halves)],
            bz[z],
        )
        for z in span
    ]

    ez = [
        (fy[z][6] + before(fy[z][6], 1) - fx[z][5] - before(fx[z][5], 0))
        for z in span
    ]
    ey = [
        (fx[z][6] + fx[down[z]][6] - fz[z][5] - before(fz[z][5], 1)) for z in span
    ]
    ex = [
        (fz[z][6] + before(fz[z][6], 0) - fy[z][5] - fy[down[z]][5]) for z in span
    ]
    result = []
    for z in span:
        def total_div(i, j, k):
            return (
                (after(fx[z][i], 1) - fx[z][i])
                + (after(fy[z][j], 0) - fy[z][j])
                + (fz[up[z]][k] - fz[z][k])
            )

        mx, my, mz = rho[z] * vx[z], rho[z] * vy[z], rho[z] * vz[z]
        energy = (
            p[z] * (1.0 / (gamma_ratio - 1.0))
            + 0.5 * (mx * vx[z] + my * vy[z] + mz * vz[z])
            + 0.5 * (cx[z] * cx[z] + cy[z] * cy[z] + cz[z] * cz[z])
        )
        result.append(
            (
                rho[z] - flux_step * total_div(0, 0, 0),
                mx - flux_step * total_div(1, 3, 2) + (time_step * 2.0 * spin_rate) * my,
                my
                - flux_step * total_div(2, 1, 3)
                - (time_step * (2.0 - shear_rate) * spin_rate) * mx,
                mz - flux_step * total_div(3, 2, 1),
                energy - flux_step * total_div(4, 4, 4),
                bx[z] - edge_step * (after(ez[z], 0) - ez[z] - (ey[up[z]] - ey[z])),
                by[z] - edge_step * (ex[up[z]] - ex[z] - (after(ez[z], 1) - ez[z])),
                bz[z] - edge_step * (after(ey[z], 1) - ey[z] - (after(ex[z], 0) - ex[z])),
            )
        )
    return result


def taken(x, index):
    return jnp.take_along_axis(x, index, axis=0, mode="promise_in_bounds")


def kernel(
    n, n_rad, planes, plasma_any, cells_any, fraction_any, box_ref, out_ref,
    block_ref, cells_ref, fraction_ref,
    gathered, from_low, from_high, packs, load_sem, send_sem, recv_sem,
    ready_sem, line_sem, near_sem, edge_ref, edge_weight_ref,
):
    fields = block_ref.shape[0]
    strip = ROWS // planes
    row_count = plasma_any.shape[2]
    total_rows = cells_ref.shape[1]
    me, row = lax.axis_index("az"), lax.axis_index("rad")
    low, high = lax.rem(row + n_rad - 1, n_rad), lax.rem(row + 1, n_rad)

    def over(first, last, body):
        lax.fori_loop(first, last, lambda peer, _: (body(peer), 0)[1], 0)

    def everywhere(body):
        if n <= 16:
            for peer in range(n):
                body(peer)
        else:
            over(0, n, body)

    loads = [
        pltpu.make_async_copy(source, target, load_sem.at[number])
        for number, (source, target) in enumerate(
            (
                (plasma_any, block_ref),
                (cells_any, cells_ref),
                (fraction_any, fraction_ref),
            )
        )
    ]
    for load in loads:
        load.start()

    barrier = pltpu.get_barrier_semaphore()

    def greet(device):
        pl.semaphore_signal(barrier, inc=1, device_id=device, device_id_type=MESH)

    at_bottom, at_top, last_peer = row == 0, row == n_rad - 1, me == n - 1

    @pl.when(at_bottom)
    def _():
        everywhere(lambda peer: greet((peer, low)))

    over(me + 1, n, lambda peer: greet((peer, row)))

    @pl.when(jnp.logical_not(at_top))
    def _():
        greet((n - 1, high))

    lane = lax.broadcasted_iota(jnp.int32, (ROWS, LANES), 1)
    line = lax.broadcasted_iota(jnp.int32, (ROWS, LANES), 0)
    box = jnp.broadcast_to(box_ref[...], (ROWS, LANES))
    for f in range(fields):
        gathered[me, f] = box
    loads[0].wait()
    apart = LANES // planes
    places = [(f, z, 4 * f + apart * z) for z in range(planes) for f in range(fields)]
    strip_lane = lane[0:strip]
    pad = jnp.zeros((strip, LANES - row_count), jnp.float32)
    block = [
        jnp.concatenate([block_ref[f, z * strip : (z + 1) * strip], pad], axis=1)
        for f, z, _ in places
    ]
    to_high = jnp.zeros((strip, LANES), jnp.float32)
    for source, (f, z, place) in zip(block, places):
        at = (strip_lane - place) & (LANES - 1)
        to_high = jnp.where(at >= LANES - 2, pltpu.roll(source, (4 + place) % LANES, 1), to_high)
    packs[1] = to_high

    greetings = me + jnp.where(at_top, n, 0) + jnp.where(last_peer & (row > 0), n, 0)

    @pl.when(greetings > 0)
    def _():
        pl.semaphore_wait(barrier, greetings)

    def tell(semaphore, device):
        pl.semaphore_signal(semaphore, inc=1, device_id=device, device_id_type=MESH)

    def send(source, target, number, device):
        pltpu.make_async_remote_copy(
            src_ref=source, dst_ref=target,
            send_sem=send_sem.at[number], recv_sem=recv_sem.at[number],
            device_id=device, device_id_type=MESH,
        ).start()

    def send_low():
        everywhere(lambda peer: send(packs.at[0], from_high.at[me], 0, (peer, low)))

    def send_high():
        everywhere(lambda peer: send(packs.at[1], from_low.at[me], 1, (peer, high)))

    def send_block(peer):
        send(gathered.at[me], gathered.at[me], 2, (peer, row))

    def send_block_later(peer):
        pl.semaphore_wait(line_sem.at[peer], 1)
        send_block(peer)

    @pl.when(at_top)
    def _():
        send_high()

    @pl.when(at_top & last_peer)
    def _():
        everywhere(lambda peer: tell(ready_sem.at[0], (peer, high)))

    @pl.when((row > 0) & last_peer)
    def _():
        everywhere(lambda peer: tell(ready_sem.at[1], (peer, low)))
        over(0, n - 1, lambda peer: tell(near_sem, (peer, row)))

    for f in range(fields):
        gathered[me, f, :, 0:row_count] = block_ref[f]
    to_low = box[0:strip]
    for source, (f, z, place) in zip(block, places):
        at = (strip_lane - place) & (LANES - 1)
        rolled = pltpu.roll(source, (LANES - 4 + place) % LANES, 1)
        to_low = jnp.where((at >= LANES - 4) & (at < LANES - 2), rolled, to_low)
    packs[0] = to_low

    over(0, me, lambda peer: tell(line_sem.at[me], (peer, row)))
    over(0, me, send_block)

    for load in loads[1:]:
        load.wait()
    cells_ref[...] = cells_ref[...] * 256 + fraction_ref[...]
    shifts = jnp.zeros((ROWS, LANES), jnp.int32)
    last = total_rows - LANES

    def loaded(start):
        return jnp.broadcast_to(cells_ref[:, start : start + LANES], (ROWS, LANES))

    for r in range(n_rad):
        start = r * row_count
        from_row = min(start, last)
        here = loaded(from_row)
        if start > from_row:
            here = pltpu.roll(here, LANES - (start - from_row), 1)
        ahead = (start + row_count) % total_rows
        behind = (start - 2) % total_rows
        for first_lane, first_row in ((row_count, ahead), (row_count + 2, behind)):
            begin = min(first_row, last)
            turn = (first_lane - (first_row - begin)) % LANES
            part = loaded(begin)
            part = pltpu.roll(part, turn, 1) if turn else part
            here = jnp.where(lane >= first_lane, part, here)
        shifts = jnp.where(row == r, here, shifts)
    circle = n * strip * 256
    below_box = (lane >= row_count + 2) & (row == 0)
    above_box = (lane >= row_count) & (lane < row_count + 2) & (row == n_rad - 1)
    edge = lane >= row_count

    def coded(total):
        total = jnp.where(total >= circle, total - circle, total)
        first = me * strip - 3 - (total >> 8)
        first = jnp.where(first < 0, first + n * strip, first)
        first = jnp.where(first < 0, first + n * strip, first)
        return first * 256 + (total & 255)

    def code_edges(offset):
        offset = offset.astype(jnp.int32)
        total = shifts + jnp.where(below_box, offset, 0) + jnp.where(above_box, circle - offset, 0)
        packed = jnp.where(edge, coded(total), 0)
        for width in (4, 8, 16, apart):
            packed = packed + pltpu.roll(packed, width, 1)
        rows, inner, next_weight = decoded(packed)
        edge_ref[0] = rows
        edge_ref[1] = inner
        edge_weight_ref[...] = next_weight

    mod_line = line & (strip - 1)
    early = line < strip

    def decoded(value):
        rows = value >> 8
        weight_next = (value & 255).astype(jnp.float32) * (1.0 / 256.0)
        return rows >> (strip.bit_length() - 1), rows & (strip - 1), weight_next

    device, inside, weight_next = decoded(coded(shifts))
    in_low = (strip_lane & 3) >= 2

    def arrived(ref, sem):
        pltpu.make_async_copy(ref, ref, sem).wait()

    over(me + 1, n, send_block_later)

    @pl.when((row > 0) & jnp.logical_not(last_peer))
    def _():
        pl.semaphore_wait(near_sem, 1)

    @pl.when(row > 0)
    def _():
        send_low()

    @pl.when(jnp.logical_not(at_top))
    def _():
        pl.semaphore_wait(ready_sem.at[1], 1)
        send_high()

    @pl.when(at_bottom)
    def _():
        pl.semaphore_wait(ready_sem.at[0], 1)
        send_low()

    others = pl.ds(0, n - 1)

    def chosen(count, where_from, load):
        def choose(e, state):
            values = load(e)
            out = []
            for d in range(3):
                hit = where_from == lax.rem(e + n - d, n)
                out.append([jnp.where(hit, v, h) for v, h in zip(values, state[d])])
            return out

        state = [[jnp.zeros(where_from.shape, jnp.float32)] * count for _ in range(3)]
        if n > 16:
            return lax.fori_loop(0, n, choose, state)
        for e in range(n):
            state = choose(e, state)
        return state

    def relocated(three, inside, weight_next):
        total = [None] * planes
        for weight, start in ((1.0 - weight_next, inside + 1), (weight_next, inside)):
            keep = mod_line >= start
            first = jnp.where(keep, three[0], three[1])
            second = jnp.where(keep, three[1], three[2])
            for z in range(planes):
                index = z * strip + ((line + start) & (strip - 1))
                part = weight * jnp.where(early, taken(first, index), taken(second, index))
                total[z] = part if total[z] is None else total[z] + part
        return total

    arrived(gathered.at[others], recv_sem.at[2])

    @pl.when(row != n_rad - 1)
    def _():
        code_edges(gathered[0, 0])

    state = chosen(fields, device, lambda e: [gathered[e, f] for f in range(fields)])
    own = [relocated([s[f] for s in state], inside, weight_next) for f in range(fields)]

    arrived(from_low, recv_sem.at[1])
    arrived(from_high, recv_sem.at[0])

    @pl.when(row == n_rad - 1)
    def _():
        spare = jnp.broadcast_to(from_high[0, 0:1], (ROWS, LANES))
        code_edges(pltpu.roll(spare, LANES - SPARE - 4, 1))

    packed_device, packed_inside, packed_weight = edge_ref[0], edge_ref[1], edge_weight_ref[...]
    state = chosen(
        1, packed_device[0:strip], lambda e: [jnp.where(in_low, from_low[e], from_high[e])]
    )
    three = [jnp.concatenate([s[0]] * planes, axis=0) for s in state]
    halo = 0.0
    for weight, start in (
        (1.0 - packed_weight, packed_inside + 1), (packed_weight, packed_inside)
    ):
        keep = mod_line >= start
        index = (line + start) & (strip - 1)
        first = taken(jnp.where(keep, three[0], three[1]), index)
        second = taken(jnp.where(keep, three[1], three[2]), index)
        halo = halo + weight * jnp.where(early, first, second)
    shifted = [
        [
            jnp.where(edge, pltpu.roll(halo, (2 * LANES - 4 * f - apart * z) % LANES, 1), own[f][z])
            for z in range(planes)
        ]
        for f in range(fields)
    ]

    result = advance(shifted, planes)
    for f in range(fields):
        for z in range(planes):
            out_ref[f, z * strip : (z + 1) * strip] = result[z][f][2 : 2 + strip]

    arrived(from_high, send_sem.at[0])
    arrived(from_low, send_sem.at[1])
    arrived(gathered.at[others], send_sem.at[2])


def body(plasma, shift_cells, shift_fraction, box_cells, box_fraction):
    fields, planes, strip, row_count = plasma.shape
    assert planes * strip == ROWS and strip + 4 == ROWS and row_count + 4 == LANES
    assert 4 * fields - 4 <= SPARE <= LANES // planes - 8
    n, n_rad = lax.axis_size("az"), lax.axis_size("rad")
    total_rows = shift_cells.shape[0]
    block_shape = (fields, ROWS, row_count)
    box = lax.cond(
        (lax.axis_index("az") == 0) & (lax.axis_index("rad") == 0),
        lambda cells, fraction: jnp.broadcast_to(cells * 256 + fraction, (LANES,)).astype(jnp.float32),
        lambda cells, fraction: jnp.zeros((LANES,), jnp.float32),
        box_cells, box_fraction,
    )
    out = pl.pallas_call(
        functools.partial(kernel, n, n_rad, planes),
        out_shape=pltpu.VMEM((fields, ROWS, LANES), jnp.float32),
        in_specs=[pl.BlockSpec(memory_space=pltpu.HBM)] * 3 + [pl.BlockSpec(memory_space=pltpu.VMEM)],
        out_specs=pl.BlockSpec(memory_space=pltpu.VMEM),
        scratch_shapes=[
            pltpu.VMEM(block_shape, jnp.float32),
            pltpu.VMEM((1, total_rows), jnp.int32),
            pltpu.VMEM((1, total_rows), jnp.int32),
            pltpu.VMEM((n, fields, ROWS, LANES), jnp.float32),
            pltpu.VMEM((n, strip, LANES), jnp.float32),
            pltpu.VMEM((n, strip, LANES), jnp.float32),
            pltpu.VMEM((2, strip, LANES), jnp.float32),
            pltpu.SemaphoreType.DMA((3,)),
            pltpu.SemaphoreType.DMA((3,)),
            pltpu.SemaphoreType.DMA((3,)),
            pltpu.SemaphoreType.REGULAR((2,)),
            pltpu.SemaphoreType.REGULAR((n,)),
            pltpu.SemaphoreType.REGULAR,
            pltpu.VMEM((2, ROWS, LANES), jnp.int32),
            pltpu.VMEM((ROWS, LANES), jnp.float32),
        ],
        compiler_params=pltpu.CompilerParams(collective_id=0, has_side_effects=True),
    )(
        plasma.reshape(block_shape),
        shift_cells.reshape(1, total_rows),
        shift_fraction.reshape(1, total_rows),
        box.reshape(1, LANES),
    )
    return out[:, :, :row_count].reshape(plasma.shape)


def solution(mesh):
    placed = (P(None, None, "az", "rad"), P(), P(), P(), P())
    return jax.shard_map(
        body, mesh=mesh, in_specs=placed, out_specs=P(None, None, "az", "rad"), check_vma=False
    )
```
